512 devices in a mesh: ctx: 64 (over z, y), mp: 8 (over x, core).
Axes of the slice: x: 4, y: 8, z: 8, core: 2. Of those that a mesh axis runs over, the one named last changes fastest.
Arguments:
- seq_in: bfloat16 [8192, 8192], P('ctx', 'mp'), may hold values from -6 to 6
- gate_in: bfloat16 [8192, 8192], P('ctx', 'mp'), may hold values from -6 to 6
- upstream: bfloat16 [8192, 8192], P('ctx', 'mp'), may hold values from -6 to 6
- forget_flags: int32 [8192], P('ctx'), may hold values 0 or 1
- conv_weight: float32 [4, 8192], P(None, 'mp'), may hold values from -3 to 3
- conv_bias: float32 [8192], P('mp'), may hold values from -3 to 3
- proj_weight: bfloat16 [8192, 544], P(('mp', 'ctx')), may hold values from -0.0625 to 0.0625
- dt_weight: bfloat16 [512, 8192], P('ctx', 'mp'), may hold values from -0.25 to 0.25
- dt_bias: float32 [8192], P('mp'), may hold values from -10 to -3
- a_log: float32 [16, 8192], P(None, 'mp'), may hold values from 0 to 2.77
- skip_gain: float32 [8192], P('mp'), may hold values from 0.5 to 1.5
Outputs:
- grad_seq: bfloat16 [8192, 8192], P('ctx', 'mp')
- grad_gate: bfloat16 [8192, 8192], P('ctx', 'mp')
- grad_dt_weight: float32 [512, 8192], P('ctx', 'mp')
- grad_conv_weight: float32 [4, 8192], P(None, ('mp', 'ctx'))
- grad_conv_bias: float32 [8192], P(('mp', 'ctx'))
- grad_dt_bias: float32 [8192], P(('mp', 'ctx'))
- grad_a_log: float32 [16, 8192], P(None, ('mp', 'ctx'))
- grad_skip: float32 [8192], P(('mp', 'ctx'))
The draws below stay inside these ranges and needn't reach their ends.
All inputs are finite; a program needn't handle non-finite values. No bound on the sum of `forget_flags` on one device may be relied on, other than what follows from the above.
Results may differ from the reference program's by a relative error of at most 0.017.
Values may be sent and summed in bfloat16 or wider, within the bound.
A program may use at most 64 MiB of HBM per device.

```python
import jax
import jax.numpy as jnp
from jax import lax

DI = 8192
STATE = 16
RANK = 512
CONV = 4
PROJ = 544
TOKENS = 8192
N_MP = 8


def place_ends(drawn, key, low, high):
    longest = drawn.shape.index(max(drawn.shape))
    spots = []
    for shift in (0, 1):
        where = [jax.random.randint(jax.random.fold_in(key, axis), (), 0, length) for axis, length in enumerate(drawn.shape)]
        where[longest] = (where[longest] + shift) % drawn.shape[longest]
        spots.append(tuple(where))
    return drawn.at[spots[0]].set(low).at[spots[1]].set(high)


def block_levels(own_key, shape, pieces, least, top_value):
    level, own = 1.0, jax.random.fold_in(own_key, 6)
    for axis_at, shards_of in pieces:
        draws = jnp.exp(jax.random.uniform(jax.random.fold_in(own, axis_at), (shards_of,), jnp.float32, least / len(pieces), top_value / len(pieces)))
        level = level * jnp.repeat(draws, shape[axis_at] // shards_of).reshape([-1 if axis == axis_at else 1 for axis in range(len(shape))])
    return level


def bell_draw(stream_key, shape, scale, bound, split=(), held_as=jnp.bfloat16):
    entries = scale * jax.random.normal(stream_key, shape, jnp.float32)
    if split:
        entries = entries * block_levels(stream_key, shape, split, -0.22, 0.18)
    return jnp.clip(entries, -bound, bound).astype(held_as)


def setup_inputs(seed: int = 0) -> dict:
    streams_of = jax.random.split(jax.random.key(seed), 12)
    return {
        "seq_in": bell_draw(streams_of[0], (TOKENS, DI), 1.0, 6.0, ((0, 64), (1, 8))),
        "gate_in": bell_draw(streams_of[1], (TOKENS, DI), 1.0, 6.0, ((0, 64), (1, 8))),
        "upstream": bell_draw(streams_of[2], (TOKENS, DI), 1.0, 6.0, ((0, 64), (1, 8))),
        "forget_flags": place_ends((jax.random.randint(streams_of[3], (TOKENS,), 0, 2) < 1).astype(jnp.int32), jax.random.fold_in(streams_of[3], 1), 0, 1),
        "conv_weight": bell_draw(streams_of[4], (CONV, DI), CONV ** -0.5, 3.0, ((1, 8),), jnp.float32),
        "conv_bias": bell_draw(streams_of[5], (DI,), 0.5, 3.0, ((0, 8),), jnp.float32),
        "proj_weight": bell_draw(streams_of[6], (DI, PROJ), DI ** -0.5, 0.0625, ((0, 512),)),
        "dt_weight": bell_draw(streams_of[7], (RANK, DI), RANK ** -0.5, 0.25, ((0, 64), (1, 8))),
        "dt_bias": jnp.clip(-10.0 + 7.0 * jax.random.uniform(streams_of[8], (DI,), jnp.float32) ** block_levels(streams_of[8], (DI,), ((0, 8),), -0.2, 0.2), -10.0, -3.0),
        "a_log": jnp.clip(2.77 * jax.random.uniform(streams_of[9], (STATE, DI), jnp.float32) ** block_levels(streams_of[9], (STATE, DI), ((1, 8),), -0.2, 0.2), 0.0, 2.77),
        "skip_gain": jnp.clip(1.0 + 0.1 * jax.random.normal(streams_of[10], (DI,), jnp.float32), 0.5, 1.5),
    }


def silu_grad(values):
    sigmoid = jax.nn.sigmoid(values)
    return sigmoid * (1.0 + values * (1.0 - sigmoid))

def split_cols(array, groups):
    shaped = array.reshape(array.shape[:-1] + (groups, array.shape[-1] // groups))
    return jnp.moveaxis(shaped, -2, 0)

def join_cols(stacked):
    moved = jnp.moveaxis(stacked, 0, -2)
    return moved.reshape(moved.shape[:-2] + (moved.shape[-2] * moved.shape[-1],))

def to_blocks(arrays):
    return tuple((a.reshape((a.shape[0] // 16, 16) + a.shape[1:]) for a in arrays))

def advance(carry, inputs):
    state, a_matrix = carry
    act_now, step_now, b_now, c_now = inputs
    state = jnp.exp(step_now[None, :] * a_matrix) * state + b_now[:, None] * (step_now * act_now)[None, :]
    return ((state, a_matrix), lax.optimization_barrier(jnp.sum(c_now[:, None] * state, axis=0)))

def run_block(carry, inputs):
    return lax.scan(advance, carry, inputs)

def scan_channels(act_full, step_size, b_matrix, c_matrix, log_rates, skip):
    a_matrix = -jnp.exp(log_rates)
    length = act_full.shape[0]
    start_state = jnp.zeros(log_rates.shape, act_full.dtype)
    carry, outputs = lax.scan(jax.checkpoint(run_block), (start_state, a_matrix), to_blocks((act_full, step_size, b_matrix, c_matrix)))
    return outputs.reshape(length, -1) + skip[None, :] * act_full

def conv_forward(seq_group, conv_group, cbias_group):
    length = seq_group.shape[0]
    padded = jnp.concatenate([jnp.zeros((CONV - 1, seq_group.shape[1]), seq_group.dtype), seq_group], axis=0)
    pre_act = jnp.zeros((length, seq_group.shape[1]), jnp.float32) + cbias_group[None, :]
    for k in range(CONV):
        pre_act = pre_act + conv_group[k][None, :] * padded[k:k + length]
    return (padded, pre_act)

def reference(seq_in, gate_in, upstream, forget_flags, conv_weight, conv_bias, proj_weight, dt_weight, dt_bias, a_log, skip_gain):
    groups = N_MP
    group_cols = DI // groups
    seq_groups = split_cols(seq_in, groups)
    gate_groups = split_cols(gate_in, groups)
    up_groups = split_cols(upstream, groups)
    conv_groups = split_cols(conv_weight, groups)
    cbias_groups = split_cols(conv_bias, groups)
    dtw_groups = split_cols(dt_weight, groups)
    dtb_groups = split_cols(dt_bias, groups)
    rate_groups = split_cols(a_log, groups)
    skip_groups = split_cols(skip_gain, groups)
    projw_groups = proj_weight.reshape(groups, group_cols, PROJ)

    def first_pass(running, inputs):
        seq_group, conv_group, cbias_group, projw_group = inputs
        padded, pre_act = conv_forward(seq_group, conv_group, cbias_group)
        act_half = jax.nn.silu(pre_act).astype(jnp.bfloat16)
        return (running + jnp.dot(act_half, projw_group, preferred_element_type=jnp.float32), None)
    projected, _ = lax.scan(first_pass, jnp.zeros((TOKENS, PROJ), jnp.float32), (seq_groups, conv_groups, cbias_groups, projw_groups))
    dt_low = projected[:, :RANK].astype(jnp.bfloat16)
    b_matrix = projected[:, RANK:RANK + STATE]
    c_matrix = projected[:, RANK + STATE:]
    flag_values = forget_flags.astype(jnp.float32)

    def second_pass(running, inputs):
        seq_group, gate_group, up_group, conv_group, cbias_group, dtw_group, dtb_group, rate_group, skip_group = inputs
        padded, pre_act = conv_forward(seq_group, conv_group, cbias_group)
        act_half = jax.nn.silu(pre_act).astype(jnp.bfloat16)
        dt_pre = jnp.dot(dt_low, dtw_group, preferred_element_type=jnp.float32) + dtb_group[None, :]
        step_size = jax.nn.softplus(dt_pre)
        mixed, pull = jax.vjp(scan_channels, act_half.astype(jnp.float32), step_size, b_matrix, c_matrix, rate_group, skip_group)
        grad_out = -flag_values[:, None] * up_group.astype(jnp.float32)
        gate_full = gate_group.astype(jnp.float32)
        grad_mixed = grad_out * jax.nn.silu(gate_full)
        grad_gate = (grad_out * mixed * silu_grad(gate_full)).astype(jnp.bfloat16)
        grad_act_scan, grad_step, grad_bmat, grad_cmat, grad_rate, grad_skip = pull(grad_mixed)
        grad_pre = grad_step * jax.nn.sigmoid(dt_pre)
        grad_pre_half = grad_pre.astype(jnp.bfloat16)
        grad_dtw = lax.dot_general(dt_low, grad_pre_half, (((0,), (0,)), ((), ())), preferred_element_type=jnp.float32)
        grad_low = lax.dot_general(grad_pre_half, dtw_group, (((1,), (1,)), ((), ())), preferred_element_type=jnp.float32)
        running = running + jnp.concatenate([grad_low, grad_bmat, grad_cmat], axis=1)
        return (running, (grad_act_scan, grad_gate, grad_dtw, lax.optimization_barrier(jnp.sum(grad_pre, axis=0)), grad_rate, grad_skip))
    grad_proj, stacked = lax.scan(second_pass, jnp.zeros((TOKENS, PROJ), jnp.float32), (seq_groups, gate_groups, up_groups, conv_groups, cbias_groups, dtw_groups, dtb_groups, rate_groups, skip_groups))
    act_grads, gate_grads, dtw_grads, dtb_grads, rate_grads, skip_grads = stacked
    grad_proj_half = grad_proj.astype(jnp.bfloat16)

    def third_pass(inputs):
        seq_group, conv_group, cbias_group, projw_group, grad_act_scan = inputs
        length = seq_group.shape[0]
        padded, pre_act = conv_forward(seq_group, conv_group, cbias_group)
        grad_act = grad_act_scan + lax.dot_general(grad_proj_half, projw_group, (((1,), (1,)), ((), ())), preferred_element_type=jnp.float32)
        grad_pre_act = grad_act * silu_grad(pre_act)
        grad_padded = jnp.concatenate([grad_pre_act, jnp.zeros((CONV - 1, seq_group.shape[1]), jnp.float32)], axis=0)
        grad_seq = jnp.zeros((length, seq_group.shape[1]), jnp.float32)
        for k in range(CONV):
            grad_seq = grad_seq + conv_group[k][None, :] * grad_padded[CONV - 1 - k:CONV - 1 - k + length]
        grad_cw = jnp.stack([lax.optimization_barrier(jnp.sum(grad_pre_act * padded[k:k + length], axis=0)) for k in range(CONV)])
        return (grad_seq.astype(jnp.bfloat16), grad_cw, lax.optimization_barrier(jnp.sum(grad_pre_act, axis=0)))
    seq_grads, cw_grads, cb_grads = lax.map(third_pass, (seq_groups, conv_groups, cbias_groups, projw_groups, act_grads))
    return (join_cols(seq_grads), join_cols(gate_grads), join_cols(dtw_grads), join_cols(cw_grads), join_cols(cb_grads), join_cols(dtb_grads), join_cols(rate_grads), join_cols(skip_grads))
```

```python
import functools

import jax
import jax.numpy as jnp
from jax import lax
from jax.experimental import pallas as pl
from jax.experimental.pallas import tpu as pltpu
from jax.sharding import PartitionSpec as P

STATE = 16
RANK = 512
CONV = 4
PROJ = RANK + 2 * STATE
LANES = 128
CHUNKS = 8
NY = 8
LOG2E = 1.4426950408889634
MESH = pl.DeviceIdType.MESH
F32, BF16 = jnp.float32, jnp.bfloat16
VMEM = pl.BlockSpec(memory_space=pltpu.VMEM)


def lanes_of(g):
    return pl.ds(pl.multiple_of(g * LANES, LANES), LANES)


def call(kernel, outs, args, scratch=(), collective=None):
    params = dict(vmem_limit_bytes=56 * 1024 * 1024)
    if collective is not None:
        params.update(collective_id=collective, has_side_effects=True)
    return pl.pallas_call(
        kernel,
        out_shape=tuple(jax.ShapeDtypeStruct(s, d) for s, d in outs),
        in_specs=[VMEM] * len(args),
        out_specs=tuple(VMEM for _ in outs),
        scratch_shapes=list(scratch),
        compiler_params=pltpu.CompilerParams(**params),
    )(*args)


def sigmoid(v):
    return 1.0 / (1.0 + jnp.exp(-v))


def where_am_i(ny):
    me = lax.axis_index("ctx")
    return me, lax.div(me, ny), lax.rem(me, ny), lax.axis_index("mp")


def greet(peers):
    barrier = pltpu.get_barrier_semaphore()
    for peer in peers:
        pl.semaphore_signal(barrier, inc=1, device_id=peer, device_id_type=MESH)
    pl.semaphore_wait(barrier, len(peers))


def push(src, dst, send, recv, peer):
    copy = pltpu.make_async_remote_copy(
        src_ref=src, dst_ref=dst, send_sem=send, recv_sem=recv, device_id=peer, device_id_type=MESH
    )
    copy.start()
    return copy


def gather_kernel(nz, ny, n_ctx, w_ref, d_ref, s_ref, wo_ref, do_ref, halo_ref, send, recv):
    me, z, y, m = where_am_i(ny)

    def y_peer(k):
        return (z * ny + lax.rem(y + k + ny, ny), m)

    def z_peer(k):
        return (lax.rem(z + k + nz, nz) * ny + y, m)

    after = (lax.rem(me + 1, n_ctx), m)
    before = (lax.rem(me + n_ctx - 1, n_ctx), m)
    greet(
        [y_peer(k) for k in range(1, ny)] + [z_peer(k) for k in range(1, nz)] + [after, before]
    )
    rows = s_ref.shape[0]
    sent = []

    def go(src, dst, slot, peer):
        copy = push(src, dst, send.at[slot], recv.at[slot], peer)
        sent.append(copy)
        return copy

    halo = go(s_ref.at[pl.ds(rows - 16, 16)], halo_ref, 0, after)
    w_first = [go(w_ref, wo_ref.at[z, y], k, y_peer(k)) for k in range(1, ny)]
    d_first = [go(d_ref, do_ref.at[z, y], 8 + k, z_peer(k)) for k in range(1, nz)]
    wo_ref[z, y] = w_ref[...]
    do_ref[z, y] = d_ref[...]

    def w_hop(k, sign, slot):
        origin = lax.rem(z - sign * (k - 1) + nz, nz)
        return go(wo_ref.at[origin], wo_ref.at[origin], slot, z_peer(sign))

    def d_hop(k, sign, slot):
        origin = lax.rem(y - sign * (k - 1) + ny, ny)
        return go(do_ref.at[:, origin], do_ref.at[:, origin], slot, y_peer(sign))

    w_right = w_left = d_right = d_left = None
    for copy in w_first:
        copy.wait_recv()
    for k in range(1, max(nz, ny) // 2 + 1):
        if w_right is not None:
            w_right.wait_recv()
        w_right = w_hop(k, 1, 16 + k) if k <= nz // 2 else None
        if w_left is not None:
            w_left.wait_recv()
        w_left = w_hop(k, -1, 24 + k) if k <= (nz - 1) // 2 else None
        if k == 1:
            for copy in d_first:
                copy.wait_recv()
        if d_right is not None:
            d_right.wait_recv()
        d_right = d_hop(k, 1, 32 + k) if k <= ny // 2 else None
        if d_left is not None:
            d_left.wait_recv()
        d_left = d_hop(k, -1, 40 + k) if k <= (ny - 1) // 2 else None
    for copy in (w_right, w_left, d_right, d_left):
        if copy is not None:
            copy.wait_recv()
    halo.wait_recv()
    for copy in sent:
        copy.wait_send()


def sum_kernel(n, p_ref, o_ref, r_ref, acc_ref, send, recv):
    me, m = lax.axis_index("ctx"), lax.axis_index("mp")

    def peer(k):
        return (me, lax.rem(m + k, n))

    greet([peer(k) for k in range(1, n)])
    first = [
        push(p_ref.at[lax.rem(m + k, n)], r_ref.at[k], send.at[k], recv.at[k], peer(k))
        for k in range(1, n)
    ]
    total = p_ref[m].astype(F32)
    for k in range(1, n):
        first[k - 1].wait_recv()
        total = total + r_ref[k].astype(F32)
    acc_ref[...] = total.astype(BF16)
    second = [
        push(acc_ref, o_ref.at[m], send.at[n + k], recv.at[n + k], peer(k)) for k in range(1, n)
    ]
    o_ref[m] = acc_ref[...]
    for copy in second:
        copy.wait_recv()
    for copy in first + second:
        copy.wait_send()


def sum_over_mp(part, n, collective):
    tokens = part.shape[0]
    shape = (n, tokens // n, PROJ)
    (out,) = call(
        functools.partial(sum_kernel, n),
        [(shape, BF16)],
        [part.reshape(shape)],
        [
            pltpu.VMEM(shape, BF16),
            pltpu.VMEM(shape[1:], BF16),
            pltpu.SemaphoreType.DMA((2 * n,)),
            pltpu.SemaphoreType.DMA((2 * n,)),
        ],
        collective,
    )
    return out.reshape(tokens, PROJ)


def split_total(total):
    high = total.astype(BF16)
    low = (total - high.astype(F32)).astype(BF16)
    shape = (CHUNKS, LANES)
    return jnp.concatenate(
        [jnp.broadcast_to(high.astype(F32), shape), jnp.broadcast_to(low.astype(F32), shape)], 0
    ).astype(BF16)


def carry_kernel(
    nz, ny, x_ref, alog_ref, o_ref, rx_ref, row_ref, rz_ref, back_ref, fw_ref, bw_ref, send, recv
):
    me, z, y, m = where_am_i(ny)

    def y_peer(k):
        return (z * ny + lax.rem(y + k, ny), m)

    def z_peer(k):
        return (lax.rem(z + k, nz) * ny + y, m)

    greet([y_peer(k) for k in range(1, ny)] + [z_peer(k) for k in range(1, nz)])
    first = [
        push(x_ref.at[lax.rem(y + k, ny)], rx_ref.at[y], send.at[k], recv.at[k], y_peer(k))
        for k in range(1, ny)
    ]
    rx_ref[y] = x_ref[y]
    a2 = -LOG2E * jnp.exp(alog_ref[y])
    for copy in first:
        copy.wait_recv()

    def total_of(block):
        tail = block[2 * STATE :].astype(F32)
        return tail[0:1] + tail[CHUNKS : CHUNKS + 1]

    zero = jnp.zeros((STATE, LANES), F32)
    totals = [total_of(rx_ref[j]) for j in range(ny)]
    forward, sums = zero, jnp.zeros((1, LANES), F32)
    before = []
    for j in range(ny):
        fw_ref[j] = forward
        before.append(sums)
        forward = jnp.exp2(a2 * totals[j]) * forward + rx_ref[j, pl.ds(0, STATE)].astype(F32)
        sums = sums + totals[j]
    backward = zero
    behind = [None] * ny
    tail_sum = jnp.zeros((1, LANES), F32)
    for j in reversed(range(ny)):
        bw_ref[j] = backward
        behind[j] = tail_sum
        backward = jnp.exp2(a2 * totals[j]) * backward + rx_ref[j, pl.ds(STATE, STATE)].astype(F32)
        tail_sum = tail_sum + totals[j]
    row_ref[pl.ds(0, STATE)] = forward.astype(BF16)
    row_ref[pl.ds(STATE, STATE)] = backward.astype(BF16)
    row_ref[pl.ds(2 * STATE, STATE)] = split_total(sums)
    second = [
        push(row_ref, rz_ref.at[z], send.at[8 + k], recv.at[8 + k], z_peer(k))
        for k in range(1, nz)
    ]
    rz_ref[z] = row_ref[...]
    for copy in second:
        copy.wait_recv()
    head, tail = zero, zero
    for k in range(nz):
        block = rz_ref[k]
        fresh = jnp.exp2(a2 * total_of(block)) * head + block[:STATE].astype(F32)
        head = jnp.where(k < z, fresh, head)
    for k in reversed(range(nz)):
        block = rz_ref[k]
        fresh = jnp.exp2(a2 * total_of(block)) * tail + block[STATE : 2 * STATE].astype(F32)
        tail = jnp.where(k > z, fresh, tail)
    for j in range(ny):
        into = fw_ref[j] + jnp.exp2(a2 * before[j]) * head
        outof = bw_ref[j] + jnp.exp2(a2 * behind[j]) * tail
        back_ref[j, pl.ds(0, STATE)] = into.astype(BF16)
        back_ref[j, pl.ds(STATE, STATE)] = outof.astype(BF16)
    third = [
        push(
            back_ref.at[lax.rem(y + k, ny)], o_ref.at[y], send.at[16 + k], recv.at[16 + k], y_peer(k)
        )
        for k in range(1, ny)
    ]
    o_ref[y] = back_ref[y]
    for copy in third:
        copy.wait_recv()
    for copy in first + second + third:
        copy.wait_send()


def scatter_kernel(
    nz,
    ny,
    n_ctx,
    dw_ref,
    sg_ref,
    head_ref,
    dwo_ref,
    sgo_ref,
    halo_ref,
    ra_ref,
    rb_ref,
    sa_ref,
    sb_ref,
    rra_ref,
    rrb_ref,
    sr_ref,
    ss_ref,
    srr_ref,
    send,
    recv,
):
    me, z, y, m = where_am_i(ny)

    def y_of(k):
        return lax.rem(y + k, ny)

    def z_of(k):
        return lax.rem(z + k, nz)

    def y_peer(k):
        return (z * ny + y_of(k), m)

    def z_peer(k):
        return (z_of(k) * ny + y, m)

    after = (lax.rem(me + 1, n_ctx), m)
    before = (lax.rem(me + n_ctx - 1, n_ctx), m)
    greet(
        [y_peer(k) for k in range(1, ny)] + [z_peer(k) for k in range(1, nz)] + [after, before]
    )
    half = dw_ref.shape[3] // 2
    sent = []

    def go(src, dst, slot, peer):
        copy = push(src, dst, send.at[slot], recv.at[slot], peer)
        sent.append(copy)
        return copy

    halo = go(head_ref, halo_ref, 0, before)
    s_first = [go(sg_ref.at[z_of(k)], sr_ref.at[k], k, z_peer(k)) for k in range(1, nz)]
    a_first = [
        go(dw_ref.at[z_of(k), :, :, pl.ds(0, half)], ra_ref.at[k], 8 + k, z_peer(k))
        for k in range(1, nz)
    ]
    b_first = [
        go(dw_ref.at[:, y_of(k), :, pl.ds(half, half)], rb_ref.at[k], 16 + k, y_peer(k))
        for k in range(1, ny)
    ]
    for copy in s_first:
        copy.wait_recv()
    total = sg_ref[z]
    for k in range(1, nz):
        total = total + sr_ref[k]
    ss_ref[...] = total
    s_second = [go(ss_ref, srr_ref.at[k], 24 + k, y_peer(k)) for k in range(1, ny)]
    for copy in a_first:
        copy.wait_recv()

    def add_a(i, carry):
        total = dw_ref[z, i, :, pl.ds(0, half)].astype(F32)
        for k in range(1, nz):
            total = total + ra_ref[k, i].astype(F32)
        sa_ref[i] = total.astype(BF16)
        return carry

    lax.fori_loop(0, ny, add_a, 0)
    a_second = [go(sa_ref.at[y_of(k)], rra_ref.at[k], 32 + k, y_peer(k)) for k in range(1, ny)]
    for copy in b_first:
        copy.wait_recv()

    def add_b(i, carry):
        total = dw_ref[i, y, :, pl.ds(half, half)].astype(F32)
        for k in range(1, ny):
            total = total + rb_ref[k, i].astype(F32)
        sb_ref[i] = total.astype(BF16)
        return carry

    lax.fori_loop(0, nz, add_b, 0)
    b_second = [go(sb_ref.at[z_of(k)], rrb_ref.at[k], 40 + k, z_peer(k)) for k in range(1, nz)]
    for copy in s_second:
        copy.wait_recv()
    total = ss_ref[...]
    for k in range(1, ny):
        total = total + srr_ref[k]
    sgo_ref[...] = total
    for copy in a_second:
        copy.wait_recv()
    total = sa_ref[y].astype(F32)
    for k in range(1, ny):
        total = total + rra_ref[k].astype(F32)
    dwo_ref[:, pl.ds(0, half)] = total
    for copy in b_second:
        copy.wait_recv()
    total = sb_ref[z].astype(F32)
    for k in range(1, nz):
        total = total + rrb_ref[k].astype(F32)
    dwo_ref[:, pl.ds(half, half)] = total
    halo.wait_recv()
    for copy in sent:
        copy.wait_send()


def permutation(tokens, transposed=False):
    row = lax.broadcasted_iota(jnp.int32, (tokens, tokens), 1 if transposed else 0)
    col = lax.broadcasted_iota(jnp.int32, (tokens, tokens), 0 if transposed else 1)
    tics = tokens // CHUNKS
    return jnp.where(col == (row & (CHUNKS - 1)) * tics + (row >> 3), 1.0, 0.0)


def dot(a, b, dims=((1,), (0,))):
    return lax.dot_general(a, b, (dims, ((), ())), preferred_element_type=F32)


def chunk_row():
    return lax.broadcasted_iota(jnp.int32, (1, CHUNKS, LANES), 1)


def with_earlier(x, edge, rim):
    last = pltpu.roll(x[x.shape[0] - rim :], 1, 1)
    last = jnp.where(chunk_row() == 0, edge[edge.shape[0] - rim :][:, None, :], last)
    return jnp.concatenate([last, x], axis=0)


def stacked(value):
    return value.reshape(value.shape[0] // CHUNKS, CHUNKS, LANES)


def flat(value):
    return value.reshape(-1, LANES)


def front_kernel(
    seq_ref,
    halo_ref,
    gate_ref,
    up_ref,
    flag_ref,
    cw_ref,
    cb_ref,
    w_ref,
    act_ref,
    pre_ref,
    g_ref,
    gg_ref,
    x_ref,
    part_ref,
    half_ref,
):
    tokens, width = seq_ref.shape
    first = lax.axis_index("ctx") == 0
    perm = permutation(tokens)
    signed = (perm * -flag_ref[...]).astype(BF16)
    perm = perm.astype(BF16)
    x_ref[...] = dot(perm, seq_ref[...])
    g_ref[...] = dot(perm, gate_ref[...])
    gg_ref[...] = dot(signed, up_ref[...])

    def group(g, carry):
        at = lanes_of(g)
        x = stacked(x_ref[:, at])
        edge = jnp.where(first, 0.0, halo_ref[:, at].astype(F32))
        padded = with_earlier(x, edge, CONV - 1)
        taps = cw_ref[:, at]
        pre = cb_ref[:, at][None] + taps[0:1][None] * padded[: x.shape[0]]
        for k in range(1, CONV):
            pre = pre + taps[k : k + 1][None] * padded[k : k + x.shape[0]]
        pre = flat(pre)
        act = (pre * sigmoid(pre)).astype(BF16)
        pre_ref[:, at] = pre
        half_ref[:, at] = act
        act_ref[:, at] = act.astype(F32)
        gate = g_ref[:, at]
        out = gg_ref[:, at]
        s = sigmoid(gate)
        g_ref[:, at] = out * (gate * s)
        gg_ref[:, at] = out * (s * (1.0 + gate * (1.0 - s)))
        return carry

    lax.fori_loop(0, width // LANES, group, 0)
    part_ref[...] = dot(half_ref[...], w_ref[...]).astype(BF16)


def spread(proj_ref, first, out_ref, tics):
    cols = proj_ref[:, pl.ds(RANK, 2 * STATE)].astype(F32)
    for n in range(STATE):
        col = cols[:, first + n : first + n + 1]
        out_ref[:, n] = stacked(jnp.broadcast_to(col, (tics * CHUNKS, LANES)))


def local_kernel(
    proj_ref,
    dt_ref,
    bias_ref,
    alog_ref,
    act_ref,
    g_ref,
    step_ref,
    sig_ref,
    pe_ref,
    pq_ref,
    x_ref,
    b_ref,
    c_ref,
    low_ref,
):
    tokens, width = act_ref.shape
    tics = tokens // CHUNKS
    pre = dot(proj_ref[:, pl.ds(0, RANK)], dt_ref[...]) + bias_ref[...]
    step_ref[...] = jnp.maximum(pre, 0.0) + jnp.log1p(jnp.exp(-jnp.abs(pre)))
    sig_ref[...] = sigmoid(pre)
    spread(proj_ref, 0, b_ref, tics)
    spread(proj_ref, STATE, c_ref, tics)
    row = chunk_row()

    def group(g, carry):
        at = lanes_of(g)
        a2 = jnp.broadcast_to(
            (-LOG2E * jnp.exp(alog_ref[:, at]))[:, None, :], (STATE, CHUNKS, LANES)
        )

        def ahead(t, carry):
            state, total = carry
            here = pl.ds(pl.multiple_of(t * CHUNKS, CHUNKS), CHUNKS)
            step = step_ref[here, at]
            flow = step * act_ref[here, at]
            state = jnp.exp2(step[None] * a2) * state + b_ref[t] * flow[None]
            return state, total + step

        zero = jnp.zeros((STATE, CHUNKS, LANES), F32)
        state, total = lax.fori_loop(
            0, tics, ahead, (zero, jnp.zeros((CHUNKS, LANES), F32)), unroll=4
        )

        def back(i, adjoint):
            t = tics - 1 - i
            here = pl.ds(pl.multiple_of(t * CHUNKS, CHUNKS), CHUNKS)
            step = step_ref[here, at]
            return jnp.exp2(step[None] * a2) * (c_ref[t] * g_ref[here, at][None] + adjoint)

        adjoint = lax.fori_loop(0, tics, back, zero, unroll=4)
        ones = jnp.exp2(total[None] * a2)
        left, right = ones, ones
        shift = 1
        while shift < CHUNKS:
            in_left = row >= shift
            in_right = row < CHUNKS - shift
            state = state + left * jnp.where(in_left, pltpu.roll(state, shift, 1), 0.0)
            left = left * jnp.where(in_left, pltpu.roll(left, shift, 1), 1.0)
            adjoint = adjoint + right * jnp.where(
                in_right, pltpu.roll(adjoint, CHUNKS - shift, 1), 0.0
            )
            right = right * jnp.where(in_right, pltpu.roll(right, CHUNKS - shift, 1), 1.0)
            shift *= 2
        pe_ref[:, :, at] = state
        pq_ref[:, :, at] = adjoint
        for n in range(STATE):
            low_ref[pl.ds(n, 1)] = state[n, CHUNKS - 1 : CHUNKS]
            low_ref[pl.ds(STATE + n, 1)] = adjoint[n, 0:1]
        x_ref[g, pl.ds(0, 2 * STATE)] = low_ref[...].astype(BF16)
        x_ref[g, pl.ds(2 * STATE, STATE)] = split_total(jnp.sum(total, axis=0, keepdims=True))
        return carry

    lax.fori_loop(0, width // LANES, group, 0)


def main_kernel(
    xin_ref,
    pe_ref,
    pq_ref,
    step_ref,
    sig_ref,
    act_ref,
    g_ref,
    gg_ref,
    proj_ref,
    alog_ref,
    skip_ref,
    dt_ref,
    gate_out,
    gas_ref,
    dw_ref,
    part_ref,
    sg_ref,
    b_ref,
    c_ref,
    h_ref,
    gb_ref,
    gc_ref,
    mix_ref,
    gpre_ref,
):
    tokens, width = act_ref.shape
    tics = tokens // CHUNKS
    spread(proj_ref, 0, b_ref, tics)
    spread(proj_ref, STATE, c_ref, tics)
    row = chunk_row()
    gb_ref[...] = jnp.zeros(gb_ref.shape, F32)
    gc_ref[...] = jnp.zeros(gc_ref.shape, F32)

    def group(g, carry):
        at = lanes_of(g)
        rates = -jnp.exp(alog_ref[:, at])
        shape = (STATE, CHUNKS, LANES)
        a1 = jnp.broadcast_to(rates[:, None, :], shape)
        a2 = a1 * LOG2E
        skip = skip_ref[:, at]
        total = jnp.sum(stacked(step_ref[:, at]), axis=0)[None]
        left, right = total, total
        shift = 1
        while shift < CHUNKS:
            left = left + jnp.where(row >= shift, pltpu.roll(left, shift, 1), 0.0)
            right = right + jnp.where(
                row < CHUNKS - shift, pltpu.roll(right, CHUNKS - shift, 1), 0.0
            )
            shift *= 2
        ends = xin_ref[g].astype(F32)
        into = jnp.broadcast_to(ends[:STATE][:, None, :], shape)
        outof = jnp.broadcast_to(ends[STATE:][:, None, :], shape)
        state = jnp.where(row >= 1, pltpu.roll(pe_ref[:, :, at], 1, 1), 0.0)
        state = state + jnp.exp2(a2 * (left - total)) * into
        adjoint = jnp.where(row < CHUNKS - 1, pltpu.roll(pq_ref[:, :, at], CHUNKS - 1, 1), 0.0)
        adjoint = adjoint + jnp.exp2(a2 * (right - total)) * outof
        h_ref[0] = state

        def ahead(t, state):
            here = pl.ds(pl.multiple_of(t * CHUNKS, CHUNKS), CHUNKS)
            step = step_ref[here, at]
            act = act_ref[here, at]
            state = jnp.exp2(step[None] * a2) * state + b_ref[t] * (step * act)[None]
            h_ref[t + 1] = state
            mixed = jnp.sum(c_ref[t] * state, axis=0) + skip * act
            mix_ref[here, at] = mixed * gg_ref[here, at]
            return state

        lax.fori_loop(0, tics, ahead, state, unroll=2)

        def back(i, carry):
            adjoint, rate_sum, pre_sum, skip_sum = carry
            t = tics - 1 - i
            here = pl.ds(pl.multiple_of(t * CHUNKS, CHUNKS), CHUNKS)
            step = step_ref[here, at]
            act = act_ref[here, at]
            grad = g_ref[here, at]
            lam = c_ref[t] * grad[None] + adjoint
            adjoint = jnp.exp2(step[None] * a2) * lam
            pull = adjoint * h_ref[t]
            gc_ref[t] += h_ref[t + 1] * grad[None]
            gb_ref[t] += lam * (step * act)[None]
            flow = jnp.sum(lam * b_ref[t], axis=0)
            slope = jnp.sum(pull * a1, axis=0)
            gas_ref[here, at] = flow * step + skip * grad
            pre = (flow * act + slope) * sig_ref[here, at]
            gpre_ref[here, at] = pre
            return (adjoint, rate_sum + pull * step[None], pre_sum + pre, skip_sum + grad * act)

        none = jnp.zeros((CHUNKS, LANES), F32)
        _, rate_sum, pre_sum, skip_sum = lax.fori_loop(
            0, tics, back, (adjoint, jnp.zeros(shape, F32), none, none)
        )
        sg_ref[g] = jnp.zeros(sg_ref.shape[1:], F32)
        sg_ref[g, pl.ds(5, 1)] = jnp.sum(pre_sum, axis=0, keepdims=True)
        sg_ref[g, pl.ds(6, 1)] = jnp.sum(skip_sum, axis=0, keepdims=True)
        rate_sum = rate_sum * a1
        for n in range(STATE):
            sg_ref[g, pl.ds(CHUNKS + n, 1)] = jnp.sum(rate_sum[n], axis=0, keepdims=True)
        return carry

    lax.fori_loop(0, width // LANES, group, 0)
    unperm = permutation(tokens, True).astype(BF16)
    gate_out[...] = dot(unperm, mix_ref[...].astype(BF16)).astype(BF16)
    half = gpre_ref[...].astype(BF16)
    low = proj_ref[:, pl.ds(0, RANK)].astype(F32)
    dw_ref[...] = dot(low.T.astype(BF16), half).astype(BF16)
    part_ref[:, pl.ds(0, RANK)] = dot(half, dt_ref[...], ((1,), (1,))).astype(BF16)
    pick = jnp.where(
        lax.broadcasted_iota(jnp.int32, (STATE * LANES, STATE), 0) // LANES
        == lax.broadcasted_iota(jnp.int32, (STATE * LANES, STATE), 1),
        1.0,
        0.0,
    ).astype(BF16)

    def folded(ref):
        side = jnp.concatenate([flat(ref[:, n]) for n in range(STATE)], axis=1)
        return dot(side.astype(BF16), pick)

    part_ref[:, pl.ds(RANK, 2 * STATE)] = jnp.concatenate(
        [folded(gb_ref), folded(gc_ref)], axis=1
    ).astype(BF16)


def tail_kernel(
    proj_ref, w_ref, gas_ref, pre_ref, x_ref, halo_ref, sg_ref, out_ref, sgo_ref, head_ref
):
    tokens, width = gas_ref.shape
    first = lax.axis_index("ctx") == 0
    out_ref[...] = dot(proj_ref[...], w_ref[...], ((1,), (1,)))

    def group(g, carry):
        at = lanes_of(g)
        pre = pre_ref[:, at]
        s = sigmoid(pre)
        grad = (gas_ref[:, at] + out_ref[:, at]) * (s * (1.0 + pre * (1.0 - s)))
        out_ref[:, at] = grad
        grad = stacked(grad)
        edge = jnp.where(first, 0.0, halo_ref[:, at].astype(F32))
        x = stacked(x_ref[:, at])
        padded = with_earlier(x, edge, CONV - 1)
        sgo_ref[g] = sg_ref[g]
        for k in range(CONV):
            part = jnp.sum(grad * padded[k : k + x.shape[0]], axis=0)
            sgo_ref[g, pl.ds(k, 1)] = jnp.sum(part, axis=0, keepdims=True)
        sgo_ref[g, pl.ds(CONV, 1)] = jnp.sum(jnp.sum(grad, axis=0), axis=0, keepdims=True)
        head_ref[:, at] = jnp.zeros((CHUNKS, LANES), F32)
        for k in range(CONV - 1):
            head_ref[pl.ds(k, 1), at] = grad[k, 0:1]
        return carry

    lax.fori_loop(0, width // LANES, group, 0)


def end_kernel(n_ctx, grad_ref, halo_ref, cw_ref, out_ref, sum_ref):
    tokens, width = grad_ref.shape
    last = lax.axis_index("ctx") == n_ctx - 1

    def group(g, carry):
        at = lanes_of(g)
        grad = stacked(grad_ref[:, at])
        edge = jnp.where(last, 0.0, halo_ref[:, at])
        later = pltpu.roll(grad[: CONV - 1], CHUNKS - 1, 1)
        later = jnp.where(chunk_row() == CHUNKS - 1, edge[: CONV - 1][:, None, :], later)
        padded = jnp.concatenate([grad, later], axis=0)
        taps = cw_ref[:, at]
        total = taps[CONV - 1 :][None] * grad
        for k in range(CONV - 1):
            off = CONV - 1 - k
            total = total + taps[k : k + 1][None] * padded[off : off + grad.shape[0]]
        sum_ref[:, at] = flat(total).astype(BF16)
        return carry

    lax.fori_loop(0, width // LANES, group, 0)
    out_ref[...] = dot(permutation(tokens, True).astype(BF16), sum_ref[...]).astype(BF16)


def body(
    ny,
    seq_in,
    gate_in,
    upstream,
    forget_flags,
    conv_weight,
    conv_bias,
    proj_weight,
    dt_weight,
    dt_bias,
    a_log,
    skip_gain,
):
    n_ctx, n_mp = lax.axis_size("ctx"), lax.axis_size("mp")
    nz = n_ctx // ny
    tokens, width = seq_in.shape
    tics = tokens // CHUNKS
    groups = width // LANES
    sems = lambda n: [pltpu.SemaphoreType.DMA((n,)), pltpu.SemaphoreType.DMA((n,))]
    full = (tokens, width)
    w_all, d_all, halo = call(
        functools.partial(gather_kernel, nz, ny, n_ctx),
        [
            ((nz, ny) + proj_weight.shape, BF16),
            ((nz, ny) + dt_weight.shape, BF16),
            ((16, width), BF16),
        ],
        [proj_weight, dt_weight, seq_in],
        sems(48),
        1,
    )
    w_all = w_all.reshape(width, PROJ)
    d_all = d_all.reshape(RANK, width)
    flags = forget_flags.astype(F32).reshape(1, tokens)
    act, pre_act, grad, gate_slope, x, part = call(
        front_kernel,
        [(full, F32)] * 5 + [((tokens, PROJ), BF16)],
        [
            seq_in,
            halo,
            gate_in,
            upstream,
            flags,
            conv_weight,
            conv_bias.reshape(1, width),
            w_all,
        ],
        [pltpu.VMEM(full, BF16)],
    )
    proj = sum_over_mp(part, n_mp, 2)
    wide = (tics, STATE, CHUNKS, LANES)
    step, sig, ends, starts, packed = call(
        local_kernel,
        [
            (full, F32),
            (full, F32),
            ((STATE, CHUNKS, width), F32),
            ((STATE, CHUNKS, width), F32),
            ((groups, 3 * STATE, LANES), BF16),
        ],
        [proj, d_all, dt_bias.reshape(1, width), a_log, act, grad],
        [pltpu.VMEM(wide, F32), pltpu.VMEM(wide, F32), pltpu.VMEM((2 * STATE, LANES), F32)],
    )
    a_blocks = a_log.reshape(STATE, groups, LANES).transpose(1, 0, 2)
    (edges,) = call(
        functools.partial(carry_kernel, nz, ny),
        [((groups, 2 * STATE, LANES), BF16)],
        [packed, a_blocks],
        [
            pltpu.VMEM((ny, 3 * STATE, LANES), BF16),
            pltpu.VMEM((3 * STATE, LANES), BF16),
            pltpu.VMEM((nz, 3 * STATE, LANES), BF16),
            pltpu.VMEM((ny, 2 * STATE, LANES), BF16),
            pltpu.VMEM((ny, STATE, LANES), F32),
            pltpu.VMEM((ny, STATE, LANES), F32),
        ]
        + sems(24),
        3,
    )
    grad_gate, grad_scan, grad_dtw, part, small = call(
        main_kernel,
        [
            (full, BF16),
            (full, F32),
            ((RANK, width), BF16),
            ((tokens, PROJ), BF16),
            ((groups, 24, LANES), F32),
        ],
        [
            edges,
            ends,
            starts,
            step,
            sig,
            act,
            grad,
            gate_slope,
            proj,
            a_log,
            skip_gain.reshape(1, width),
            d_all,
        ],
        [
            pltpu.VMEM(wide, F32),
            pltpu.VMEM(wide, F32),
            pltpu.VMEM((tics + 1,) + wide[1:], F32),
            pltpu.VMEM(wide, F32),
            pltpu.VMEM(wide, F32),
            pltpu.VMEM(full, F32),
            pltpu.VMEM(full, F32),
        ],
    )
    grad_proj = sum_over_mp(part, n_mp, 4)
    grad_pre_act, small, head = call(
        tail_kernel,
        [(full, F32), ((groups, 24, LANES), F32), ((CHUNKS, width), F32)],
        [grad_proj, w_all, grad_scan, pre_act, x, halo, small],
    )
    rows = dt_weight.shape[0]
    half = width // 2
    grad_dtw, small, later = call(
        functools.partial(scatter_kernel, nz, ny, n_ctx),
        [((rows, width), F32), ((24, LANES), F32), ((CHUNKS, width), F32)],
        [grad_dtw.reshape(nz, ny, rows, width), small, head],
        [
            pltpu.VMEM((nz, ny, rows, half), BF16),
            pltpu.VMEM((ny, nz, rows, half), BF16),
            pltpu.VMEM((ny, rows, half), BF16),
            pltpu.VMEM((nz, rows, half), BF16),
            pltpu.VMEM((ny, rows, half), BF16),
            pltpu.VMEM((nz, rows, half), BF16),
            pltpu.VMEM((nz, 24, LANES), F32),
            pltpu.VMEM((24, LANES), F32),
            pltpu.VMEM((ny, 24, LANES), F32),
        ]
        + sems(48),
        5,
    )
    (grad_seq,) = call(
        functools.partial(end_kernel, n_ctx),
        [(full, BF16)],
        [grad_pre_act, later, conv_weight],
        [pltpu.VMEM(full, BF16)],
    )
    share = LANES // ny
    mine = lax.dynamic_slice_in_dim(small, lax.rem(lax.axis_index("ctx"), ny) * share, share, 1)
    return (
        grad_seq,
        grad_gate,
        grad_dtw,
        mine[:CONV],
        mine[CONV],
        mine[5],
        mine[8:],
        mine[6],
    )


def build(mesh, ny):
    return jax.shard_map(
        functools.partial(body, ny),
        mesh=mesh,
        in_specs=(
            P("ctx", "mp"),
            P("ctx", "mp"),
            P("ctx", "mp"),
            P("ctx"),
            P(None, "mp"),
            P("mp"),
            P(("mp", "ctx"), None),
            P("ctx", "mp"),
            P("mp"),
            P(None, "mp"),
            P("mp"),
        ),
        out_specs=(
            P("ctx", "mp"),
            P("ctx", "mp"),
            P("ctx", "mp"),
            P(None, ("mp", "ctx")),
            P(("mp", "ctx")),
            P(("mp", "ctx")),
            P(None, ("mp", "ctx")),
            P(("mp", "ctx")),
        ),
        check_vma=False,
    )


def solution(mesh):
    return build(mesh, NY)
```

```python
import functools

import jax
import jax.numpy as jnp
from jax import lax
from jax.experimental import pallas as pl
from jax.experimental.pallas import tpu as pltpu
from jax.sharding import PartitionSpec as P

STATE = 16
RANK = 512
CONV = 4
PROJ = RANK + 2 * STATE
LANES = 128
CHUNKS = 8
NY = 8
LOG2E = 1.4426950408889634
MESH = pl.DeviceIdType.MESH
F32, BF16 = jnp.float32, jnp.bfloat16
VMEM = pl.BlockSpec(memory_space=pltpu.VMEM)


def lanes_of(g):
    return pl.ds(pl.multiple_of(g * LANES, LANES), LANES)


def call(kernel, outs, args, scratch=(), collective=None):
    params = dict(vmem_limit_bytes=56 * 1024 * 1024)
    if collective is not None:
        params.update(collective_id=collective, has_side_effects=True)
    return pl.pallas_call(
        kernel,
        out_shape=tuple(jax.ShapeDtypeStruct(s, d) for s, d in outs),
        in_specs=[VMEM] * len(args),
        out_specs=tuple(VMEM for _ in outs),
        scratch_shapes=list(scratch),
        compiler_params=pltpu.CompilerParams(**params),
    )(*args)


def sigmoid(v):
    return 1.0 / (1.0 + jnp.exp(-v))


def split_total(total):
    high = total.astype(BF16)
    low = (total - high.astype(F32)).astype(BF16)
    shape = (CHUNKS, LANES)
    return jnp.concatenate(
        [jnp.broadcast_to(high.astype(F32), shape), jnp.broadcast_to(low.astype(F32), shape)], 0
    ).astype(BF16)


def permutation(tokens, transposed=False):
    row = lax.broadcasted_iota(jnp.int32, (tokens, tokens), 1 if transposed else 0)
    col = lax.broadcasted_iota(jnp.int32, (tokens, tokens), 0 if transposed else 1)
    tics = tokens // CHUNKS
    return jnp.where(col == (row & (CHUNKS - 1)) * tics + (row >> 3), 1.0, 0.0)


def dot(a, b, dims=((1,), (0,))):
    return lax.dot_general(a, b, (dims, ((), ())), preferred_element_type=F32)


def chunk_row():
    return lax.broadcasted_iota(jnp.int32, (1, CHUNKS, LANES), 1)


def with_earlier(x, edge, rim):
    last = pltpu.roll(x[x.shape[0] - rim :], 1, 1)
    last = jnp.where(chunk_row() == 0, edge[edge.shape[0] - rim :][:, None, :], last)
    return jnp.concatenate([last, x], axis=0)


def stacked(value):
    return value.reshape(value.shape[0] // CHUNKS, CHUNKS, LANES)


def flat(value):
    return value.reshape(-1, LANES)


class Net:
    def __init__(self, nz, ny, n_ctx, n_mp, send, recv):
        self.nz, self.ny, self.n_ctx, self.n_mp = nz, ny, n_ctx, n_mp
        self.send, self.recv = send, recv
        self.me, self.m = lax.axis_index("ctx"), lax.axis_index("mp")
        self.z, self.y = lax.div(self.me, ny), lax.rem(self.me, ny)
        self.slots, self.started = 0, []

    def y_of(self, k):
        return lax.rem(self.y + k + self.ny, self.ny)

    def z_of(self, k):
        return lax.rem(self.z + k + self.nz, self.nz)

    def m_of(self, k):
        return lax.rem(self.m + k, self.n_mp)

    def at_y(self, k):
        return (self.z * self.ny + self.y_of(k), self.m)

    def at_z(self, k):
        return (self.z_of(k) * self.ny + self.y, self.m)

    def at_m(self, k):
        return (self.me, self.m_of(k))

    def at_ctx(self, k):
        return (lax.rem(self.me + k + self.n_ctx, self.n_ctx), self.m)

    def greet(self):
        barrier = pltpu.get_barrier_semaphore()
        peers = [self.at_y(k) for k in range(1, self.ny)]
        peers += [self.at_z(k) for k in range(1, self.nz)]
        peers += [self.at_m(k) for k in range(1, self.n_mp)]
        peers += [self.at_ctx(1), self.at_ctx(-1)]
        for peer in peers:
            pl.semaphore_signal(barrier, inc=1, device_id=peer, device_id_type=MESH)
        return lambda: pl.semaphore_wait(barrier, len(peers))

    def take(self, count):
        first = self.slots
        self.slots += count
        return first

    def copy(self, src, dst, slot, peer):
        return pltpu.make_async_remote_copy(
            src_ref=src,
            dst_ref=dst,
            send_sem=self.send.at[slot],
            recv_sem=self.recv.at[slot],
            device_id=peer,
            device_id_type=MESH,
        )

    def go(self, src, dst, peer):
        made = self.copy(src, dst, self.take(1), peer)
        made.start()
        self.started.append(made)
        return made

    def finish(self):
        for made in self.started:
            made.wait_send()


def arrived(copies):
    for made in copies:
        made.wait_recv()


def ring_start(net, size, place, peer, part):
    if size != 8:
        return [net.go(part(place(0), 2), part(place(0), 2), peer(k)) for k in range(1, size)]
    return [net.go(part(place(0), 2), part(place(0), 2), peer(k)) for k in (2, -2, 1, -1)]


def ring_relay(net, size, place, peer, part, first):
    if size != 8:
        arrived(first)
        return []
    arrived(first[:2])
    made = [
        net.go(part(place(-2), 0), part(place(-2), 0), peer(2)),
        net.go(part(place(2), 1), part(place(2), 1), peer(-2)),
        net.go(part(place(-2), 2), part(place(-2), 2), peer(1)),
        net.go(part(place(2), 2), part(place(2), 2), peer(-1)),
    ]
    return made


def cut(ref, size, axis, lanes):
    def part(origin, which):
        span = pl.ds(0, size) if which == 2 else pl.ds(which * (size // 2), size // 2)
        if axis == "z":
            return ref.at[origin, span, :, lanes]
        return ref.at[span, origin, :, lanes]

    return part


def mega_kernel(nz, ny, n_ctx, n_mp, names, *refs):
    r = dict(zip(names, refs))
    net = Net(nz, ny, n_ctx, n_mp, r["send"], r["recv"])
    z, y, m = net.z, net.y, net.m
    seq_ref, alog_ref, skip_ref = r["seq"], r["alog"], r["skip"]
    tokens, width = seq_ref.shape
    tics, groups = tokens // CHUNKS, width // LANES
    half_width = width // 2
    row = chunk_row()
    met = net.greet()

    perm = permutation(tokens)
    signed = (perm * -r["flag"][...].astype(F32)).astype(BF16)
    perm = perm.astype(BF16)
    g_ref, gg_ref, x_ref = r["g"], r["gg"], r["x"]
    x_ref[...] = dot(perm, seq_ref[...])
    g_ref[...] = dot(perm, r["gate"][...])
    gg_ref[...] = dot(signed, r["up"][...])
    wo_ref, do_ref = r["w_all"], r["d_all"]
    wo_ref[z, y] = r["w"][...]
    do_ref[z, y] = r["d"][...]
    met()

    w_cut = 2 * LANES
    w_lo, w_hi = pl.ds(0, w_cut), pl.ds(w_cut, PROJ - w_cut)
    d_lo, d_hi = pl.ds(0, half_width), pl.ds(half_width, half_width)
    halo = net.go(seq_ref.at[pl.ds(tokens - 16, 16)], r["halo"], net.at_ctx(1))

    def first_leg(src, ref, lo, hi):
        a = [net.go(src.at[:, lo], ref.at[z, y, :, lo], net.at_y(k)) for k in range(1, ny)]
        b = [net.go(src.at[:, hi], ref.at[z, y, :, hi], net.at_z(k)) for k in range(1, nz)]
        return a, b

    w_a, w_b = first_leg(r["w"], wo_ref, w_lo, w_hi)
    halo.wait_recv()
    first_block = net.me == 0
    act_ref, pre_ref, actb_ref = r["act"], r["pre"], r["actb"]

    def conv(g, carry):
        at = lanes_of(g)
        x = stacked(x_ref[:, at])
        edge = jnp.where(first_block, 0.0, r["halo"][:, at].astype(F32))
        padded = with_earlier(x, edge, CONV - 1)
        taps = r["cw"][:, at]
        pre = r["cb"][:, at][None] + taps[0:1][None] * padded[: x.shape[0]]
        for k in range(1, CONV):
            pre = pre + taps[k : k + 1][None] * padded[k : k + x.shape[0]]
        pre = flat(pre)
        act = (pre * sigmoid(pre)).astype(BF16)
        pre_ref[:, at] = pre
        actb_ref[:, at] = act
        act_ref[:, at] = act.astype(F32)
        return carry

    lax.fori_loop(0, groups, conv, 0)

    def legs(ref, lo, hi):
        return (
            (nz, net.z_of, net.at_z, cut(ref, ny, "z", lo)),
            (ny, net.y_of, net.at_y, cut(ref, nz, "y", hi)),
        )

    w_za, w_yb = legs(wo_ref, w_lo, w_hi)
    arrived(w_a)
    w_a = ring_start(net, *w_za)
    arrived(w_b)
    w_b = ring_start(net, *w_yb)
    d_a, d_b = first_leg(r["d"], do_ref, d_lo, d_hi)

    def gates(g, carry):
        at = lanes_of(g)
        gate = g_ref[:, at]
        out = gg_ref[:, at]
        s = sigmoid(gate)
        g_ref[:, at] = out * (gate * s)
        gg_ref[:, at] = out * (s * (1.0 + gate * (1.0 - s)))
        return carry

    lax.fori_loop(0, groups, gates, 0)
    w_a2 = ring_relay(net, *w_za, w_a)
    w_b2 = ring_relay(net, *w_yb, w_b)
    d_za, d_yb = legs(do_ref, d_lo, d_hi)
    arrived(d_a)
    d_a = ring_start(net, *d_za)
    arrived(d_b)
    d_b = ring_start(net, *d_yb)
    if nz == 8:
        arrived(w_a[2:])
    if ny == 8:
        arrived(w_b[2:])
    arrived(w_a2 + w_b2)

    sum_shape = (n_mp, tokens // n_mp, PROJ)
    w_full = wo_ref[...].reshape(width, PROJ)
    r["p1"][...] = dot(actb_ref[...], w_full).astype(BF16).reshape(sum_shape)

    def sum_start(p_ref, r_ref):
        return [net.go(p_ref.at[net.m_of(k)], r_ref.at[k], net.at_m(k)) for k in range(1, n_mp)]

    def sum_turn(first, p_ref, r_ref, acc_ref, o_ref):
        total = p_ref[m].astype(F32)
        for k in range(1, n_mp):
            first[k - 1].wait_recv()
            total = total + r_ref[k].astype(F32)
        acc_ref[...] = total.astype(BF16)
        o_ref[m] = acc_ref[...]
        return [net.go(acc_ref, o_ref.at[m], net.at_m(k)) for k in range(1, n_mp)]

    s1 = sum_start(r["p1"], r["q1"])
    d_a2 = ring_relay(net, *d_za, d_a)
    d_b2 = ring_relay(net, *d_yb, d_b)
    s2 = sum_turn(s1, r["p1"], r["q1"], r["acc1"], r["proj"])
    if nz == 8:
        arrived(d_a[2:])
    if ny == 8:
        arrived(d_b[2:])
    arrived(d_a2 + d_b2)

    def lay_out(i, carry):
        rows = do_ref.shape[2] * ny
        block = do_ref[i].astype(F32).reshape(rows, width)
        r["dt"][pl.ds(pl.multiple_of(i * rows, rows), rows)] = block.astype(BF16)
        return carry

    lax.fori_loop(0, nz, lay_out, 0)
    dt_ref = r["dt"]
    arrived(s2)

    proj = r["proj"][...].reshape(tokens, PROJ)
    low = proj[:, :RANK]
    cols = proj[:, RANK:].astype(F32)
    r["low_t"][...] = low.astype(F32).T.astype(BF16)
    step_ref, sig_ref = r["step"], r["sig"]
    step_ref[...] = dot(low, dt_ref[...])
    b_ref, c_ref = r["b"], r["c"]

    def spread(first, out_ref):
        for n in range(STATE):
            col = cols[:, first + n : first + n + 1]
            out_ref[:, n] = stacked(jnp.broadcast_to(col, (tokens, LANES)))

    spread(0, b_ref)
    spread(STATE, c_ref)
    pe_ref, pq_ref, pack_ref, ends_ref = r["pe"], r["pq"], r["pack"], r["ends"]
    wide = (STATE, CHUNKS, LANES)

    def here_of(t):
        return pl.ds(pl.multiple_of(t * CHUNKS, CHUNKS), CHUNKS)

    def local(g, carry):
        at = lanes_of(g)
        pre = step_ref[:, at] + r["dbias"][:, at]
        step_ref[:, at] = jnp.maximum(pre, 0.0) + jnp.log1p(jnp.exp(-jnp.abs(pre)))
        sig_ref[:, at] = sigmoid(pre)
        a2 = jnp.broadcast_to((-LOG2E * jnp.exp(alog_ref[:, at]))[:, None, :], wide)

        def ahead(t, carry):
            state, total = carry
            here = here_of(t)
            step = step_ref[here, at]
            flow = step * act_ref[here, at]
            state = jnp.exp2(step[None] * a2) * state + b_ref[t] * flow[None]
            return state, total + step

        zero = jnp.zeros(wide, F32)
        state, total = lax.fori_loop(
            0, tics, ahead, (zero, jnp.zeros((CHUNKS, LANES), F32)), unroll=4
        )

        def back(i, adjoint):
            t = tics - 1 - i
            here = here_of(t)
            step = step_ref[here, at]
            return jnp.exp2(step[None] * a2) * (c_ref[t] * g_ref[here, at][None] + adjoint)

        adjoint = lax.fori_loop(0, tics, back, zero, unroll=4)
        left = jnp.exp2(total[None] * a2)
        right = left
        shift = 1
        while shift < CHUNKS:
            in_left = row >= shift
            in_right = row < CHUNKS - shift
            state = state + left * jnp.where(in_left, pltpu.roll(state, shift, 1), 0.0)
            left = left * jnp.where(in_left, pltpu.roll(left, shift, 1), 1.0)
            adjoint = adjoint + right * jnp.where(
                in_right, pltpu.roll(adjoint, CHUNKS - shift, 1), 0.0
            )
            right = right * jnp.where(in_right, pltpu.roll(right, CHUNKS - shift, 1), 1.0)
            shift *= 2
        pe_ref[:, :, at] = state
        pq_ref[:, :, at] = adjoint
        for n in range(STATE):
            ends_ref[pl.ds(n, 1)] = state[n, CHUNKS - 1 : CHUNKS]
            ends_ref[pl.ds(STATE + n, 1)] = adjoint[n, 0:1]
        pack_ref[g, pl.ds(0, 2 * STATE)] = ends_ref[...].astype(BF16)
        pack_ref[g, pl.ds(2 * STATE, STATE)] = split_total(jnp.sum(total, axis=0, keepdims=True))
        return carry

    lax.fori_loop(0, groups, local, 0)

    rx_ref, row_ref, rz_ref, back_ref, edge_ref = r["rx"], r["rowt"], r["rz"], r["backt"], r["edges"]
    fw_ref, bw_ref = r["fw"], r["bw"]
    c1 = [net.go(pack_ref.at[net.y_of(k)], rx_ref.at[y], net.at_y(k)) for k in range(1, ny)]
    rx_ref[y] = pack_ref[y]
    my_a2 = -LOG2E * jnp.exp(alog_ref[:, lanes_of(y)])
    gb_ref, gc_ref = r["gb"], r["gc"]
    gb_ref[...] = jnp.zeros(gb_ref.shape, F32)
    gc_ref[...] = jnp.zeros(gc_ref.shape, F32)
    arrived(c1)

    def total_of(block):
        tail = block[2 * STATE :].astype(F32)
        return tail[0:1] + tail[CHUNKS : CHUNKS + 1]

    zero = jnp.zeros((STATE, LANES), F32)
    totals = [total_of(rx_ref[j]) for j in range(ny)]
    forward, sums = zero, jnp.zeros((1, LANES), F32)
    before, behind = [], [None] * ny
    for j in range(ny):
        fw_ref[j] = forward
        before.append(sums)
        forward = jnp.exp2(my_a2 * totals[j]) * forward + rx_ref[j, pl.ds(0, STATE)].astype(F32)
        sums = sums + totals[j]
    backward, tail_sum = zero, jnp.zeros((1, LANES), F32)
    for j in reversed(range(ny)):
        bw_ref[j] = backward
        behind[j] = tail_sum
        backward = jnp.exp2(my_a2 * totals[j]) * backward + rx_ref[j, pl.ds(STATE, STATE)].astype(F32)
        tail_sum = tail_sum + totals[j]
    row_ref[pl.ds(0, STATE)] = forward.astype(BF16)
    row_ref[pl.ds(STATE, STATE)] = backward.astype(BF16)
    row_ref[pl.ds(2 * STATE, STATE)] = split_total(sums)
    c2 = [net.go(row_ref, rz_ref.at[z], net.at_z(k)) for k in range(1, nz)]
    rz_ref[z] = row_ref[...]
    arrived(c2)
    head, tail = zero, zero
    for k in range(nz):
        block = rz_ref[k]
        fresh = jnp.exp2(my_a2 * total_of(block)) * head + block[:STATE].astype(F32)
        head = jnp.where(k < z, fresh, head)
    for k in reversed(range(nz)):
        block = rz_ref[k]
        fresh = jnp.exp2(my_a2 * total_of(block)) * tail + block[STATE : 2 * STATE].astype(F32)
        tail = jnp.where(k > z, fresh, tail)
    for j in range(ny):
        into = fw_ref[j] + jnp.exp2(my_a2 * before[j]) * head
        outof = bw_ref[j] + jnp.exp2(my_a2 * behind[j]) * tail
        back_ref[j, pl.ds(0, STATE)] = into.astype(BF16)
        back_ref[j, pl.ds(STATE, STATE)] = outof.astype(BF16)
    c3 = [net.go(back_ref.at[net.y_of(k)], edge_ref.at[y], net.at_y(k)) for k in range(1, ny)]
    edge_ref[y] = back_ref[y]
    arrived(c3)

    h_ref, mix_ref, gpre_ref, half_ref = r["h"], r["mix"], r["gpre"], r["half"]
    gas_ref, dw_ref, ra_ref, sg_ref = r["gas"], r["dw"], r["ra"], r["sg"]
    base = net.take(groups * 8)

    def dw_copy(g, k, along_z):
        at = lanes_of(g)
        if along_z:
            src, peer = dw_ref.at[net.z_of(k), :, :, at], net.at_z(k)
        else:
            src, peer = dw_ref.at[:, net.y_of(k), :, at], net.at_y(k)
        return net.copy(src, ra_ref.at[k, :, :, at], base + g * 8 + k, peer)

    def main(i, carry):
        g = lax.rem(i, 2) * (groups // 2) + lax.div(i, 2)
        at = lanes_of(g)
        rates = -jnp.exp(alog_ref[:, at])
        a1 = jnp.broadcast_to(rates[:, None, :], wide)
        a2 = a1 * LOG2E
        skip = skip_ref[:, at]
        total = jnp.sum(stacked(step_ref[:, at]), axis=0)[None]
        left, right = total, total
        shift = 1
        while shift < CHUNKS:
            left = left + jnp.where(row >= shift, pltpu.roll(left, shift, 1), 0.0)
            right = right + jnp.where(
                row < CHUNKS - shift, pltpu.roll(right, CHUNKS - shift, 1), 0.0
            )
            shift *= 2
        ends = edge_ref[g].astype(F32)
        into = jnp.broadcast_to(ends[:STATE][:, None, :], wide)
        outof = jnp.broadcast_to(ends[STATE:][:, None, :], wide)
        state = jnp.where(row >= 1, pltpu.roll(pe_ref[:, :, at], 1, 1), 0.0)
        state = state + jnp.exp2(a2 * (left - total)) * into
        adjoint = jnp.where(row < CHUNKS - 1, pltpu.roll(pq_ref[:, :, at], CHUNKS - 1, 1), 0.0)
        adjoint = adjoint + jnp.exp2(a2 * (right - total)) * outof
        h_ref[0] = state

        def ahead(t, state):
            here = here_of(t)
            step = step_ref[here, at]
            act = act_ref[here, at]
            state = jnp.exp2(step[None] * a2) * state + b_ref[t] * (step * act)[None]
            h_ref[t + 1] = state
            mixed = jnp.sum(c_ref[t] * state, axis=0) + skip * act
            mix_ref[here] = mixed * gg_ref[here, at]
            return state

        lax.fori_loop(0, tics, ahead, state, unroll=2)
        r["mixo"][:, at] = mix_ref[...].astype(BF16)

        def back(i, carry):
            adjoint, rate_sum, pre_sum, skip_sum = carry
            t = tics - 1 - i
            here = here_of(t)
            step = step_ref[here, at]
            act = act_ref[here, at]
            grad = g_ref[here, at]
            lam = c_ref[t] * grad[None] + adjoint
            adjoint = jnp.exp2(step[None] * a2) * lam
            pull = adjoint * h_ref[t]
            gc_ref[t] += h_ref[t + 1] * grad[None]
            gb_ref[t] += lam * (step * act)[None]
            flow = jnp.sum(lam * b_ref[t], axis=0)
            slope = jnp.sum(pull * a1, axis=0)
            gas_ref[here, at] = flow * step + skip * grad
            pre = (flow * act + slope) * sig_ref[here, at]
            gpre_ref[here] = pre
            return (adjoint, rate_sum + pull * step[None], pre_sum + pre, skip_sum + grad * act)

        none = jnp.zeros((CHUNKS, LANES), F32)
        _, rate_sum, pre_sum, skip_sum = lax.fori_loop(
            0, tics, back, (adjoint, jnp.zeros(wide, F32), none, none)
        )
        half = gpre_ref[...].astype(BF16)
        half_ref[:, at] = half
        dw_ref[:, :, :, at] = (
            dot(r["low_t"][...], half).reshape(dw_ref.shape[:3] + (LANES,)).astype(BF16)
        )

        @pl.when(g < groups // 2)
        def _():
            for k in range(1, nz):
                dw_copy(g, k, True).start()

        @pl.when(g >= groups // 2)
        def _():
            for k in range(1, ny):
                dw_copy(g, k, False).start()

        sg_ref[g] = jnp.zeros(sg_ref.shape[1:], F32)
        sg_ref[g, pl.ds(5, 1)] = jnp.sum(pre_sum, axis=0, keepdims=True)
        sg_ref[g, pl.ds(6, 1)] = jnp.sum(skip_sum, axis=0, keepdims=True)
        rate_sum = rate_sum * a1
        for n in range(STATE):
            sg_ref[g, pl.ds(CHUNKS + n, 1)] = jnp.sum(rate_sum[n], axis=0, keepdims=True)
        return carry

    lax.fori_loop(0, groups, main, 0)

    pick = jnp.where(
        lax.broadcasted_iota(jnp.int32, (STATE * LANES, STATE), 0) // LANES
        == lax.broadcasted_iota(jnp.int32, (STATE * LANES, STATE), 1),
        1.0,
        0.0,
    ).astype(BF16)

    def folded(ref):
        side = jnp.concatenate([flat(ref[:, n]) for n in range(STATE)], axis=1)
        return dot(side.astype(BF16), pick)

    r["p2"][:, :, pl.ds(0, RANK)] = (
        dot(half_ref[...], dt_ref[...], ((1,), (1,))).astype(BF16).reshape(sum_shape[:2] + (RANK,))
    )
    r["p2"][:, :, pl.ds(RANK, 2 * STATE)] = (
        jnp.concatenate([folded(gb_ref), folded(gc_ref)], axis=1)
        .astype(BF16)
        .reshape(sum_shape[:2] + (2 * STATE,))
    )
    s3 = sum_start(r["p2"], r["q2"])
    sa_ref, sb_ref, rra_ref, rrb_ref = r["sa"], r["sb"], r["rra"], r["rrb"]
    lo, hi = pl.ds(0, half_width), pl.ds(half_width, half_width)
    half_groups = groups // 2

    def add_a(i, carry):
        total = dw_ref[z, i, :, lo].astype(F32)
        for k in range(1, nz):
            total = total + ra_ref[k, i, :, lo].astype(F32)
        sa_ref[i] = total.astype(BF16)
        return carry

    def add_b(i, carry):
        total = dw_ref[i, y, :, hi].astype(F32)
        for k in range(1, ny):
            total = total + ra_ref[k, i, :, hi].astype(F32)
        sb_ref[i] = total.astype(BF16)
        return carry

    s4 = sum_turn(s3, r["p2"], r["q2"], r["acc2"], r["gproj"])
    arrived([dw_copy(g, k, True) for g in range(half_groups) for k in range(1, nz)])
    lax.fori_loop(0, ny, add_a, 0)
    a2nd = [net.go(sa_ref.at[net.y_of(k)], rra_ref.at[k], net.at_y(k)) for k in range(1, ny)]
    arrived([dw_copy(g, k, False) for g in range(half_groups, groups) for k in range(1, ny)])
    lax.fori_loop(0, nz, add_b, 0)
    b2nd = [net.go(sb_ref.at[net.z_of(k)], rrb_ref.at[k], net.at_z(k)) for k in range(1, nz)]
    arrived(s4)

    out_ref, head_ref = r["grad"], r["head"]
    out_ref[...] = dot(r["gproj"][...].reshape(tokens, PROJ), wo_ref[...].reshape(width, PROJ), ((1,), (1,)))

    def close(g, carry):
        at = lanes_of(g)
        pre = pre_ref[:, at]
        s = sigmoid(pre)
        grad = (gas_ref[:, at] + out_ref[:, at]) * (s * (1.0 + pre * (1.0 - s)))
        out_ref[:, at] = grad
        grad = stacked(grad)
        edge = jnp.where(first_block, 0.0, r["halo"][:, at].astype(F32))
        x = stacked(x_ref[:, at])
        padded = with_earlier(x, edge, CONV - 1)
        for k in range(CONV):
            part = jnp.sum(grad * padded[k : k + x.shape[0]], axis=0)
            sg_ref[g, pl.ds(k, 1)] = jnp.sum(part, axis=0, keepdims=True)
        sg_ref[g, pl.ds(CONV, 1)] = jnp.sum(jnp.sum(grad, axis=0), axis=0, keepdims=True)
        head_ref[:, at] = jnp.zeros((CHUNKS, LANES), F32)
        for k in range(CONV - 1):
            head_ref[pl.ds(k, 1), at] = grad[k, 0:1]
        return carry

    lax.fori_loop(0, groups, close, 0)
    t1 = [net.go(sg_ref.at[net.z_of(k)], r["sr"].at[k], net.at_z(k)) for k in range(1, nz)]
    later = net.go(head_ref, r["later"], net.at_ctx(-1))
    arrived(a2nd)
    total = sa_ref[y].astype(F32)
    for k in range(1, ny):
        total = total + rra_ref[k].astype(F32)
    r["dwo"][:, lo] = total
    arrived(b2nd)
    total = sb_ref[z].astype(F32)
    for k in range(1, nz):
        total = total + rrb_ref[k].astype(F32)
    r["dwo"][:, hi] = total
    arrived(t1)
    total = sg_ref[z]
    for k in range(1, nz):
        total = total + r["sr"][k]
    r["ss"][...] = total
    t2 = [net.go(r["ss"], r["srr"].at[k], net.at_y(k)) for k in range(1, ny)]
    later.wait_recv()
    arrived(t2)
    total = r["ss"][...]
    for k in range(1, ny):
        total = total + r["srr"][k]
    r["smallo"][...] = total
    for g in range(groups):
        along_z = g < half_groups
        for k in range(1, nz if along_z else ny):
            dw_copy(g, k, along_z).wait_send()
    net.finish()


def end_kernel(
    n_ctx,
    ny,
    grad_ref,
    halo_ref,
    cw_ref,
    mix_ref,
    dwo_ref,
    small_ref,
    out_ref,
    gate_ref,
    dw_ref,
    w_ref,
    b_ref,
    t_ref,
    a_ref,
    s_ref,
    sum_ref,
):
    tokens, width = grad_ref.shape
    me = lax.axis_index("ctx")
    last = me == n_ctx - 1

    def group(g, carry):
        at = lanes_of(g)
        grad = stacked(grad_ref[:, at])
        edge = jnp.where(last, 0.0, halo_ref[:, at])
        later = pltpu.roll(grad[: CONV - 1], CHUNKS - 1, 1)
        later = jnp.where(chunk_row() == CHUNKS - 1, edge[: CONV - 1][:, None, :], later)
        padded = jnp.concatenate([grad, later], axis=0)
        taps = cw_ref[:, at]
        total = taps[CONV - 1 :][None] * grad
        for k in range(CONV - 1):
            off = CONV - 1 - k
            total = total + taps[k : k + 1][None] * padded[off : off + grad.shape[0]]
        sum_ref[:, at] = flat(total).astype(BF16)
        return carry

    lax.fori_loop(0, width // LANES, group, 0)
    unperm = permutation(tokens, True).astype(BF16)
    out_ref[...] = dot(unperm, sum_ref[...]).astype(BF16)
    gate_ref[...] = dot(unperm, mix_ref[...]).astype(BF16)
    dw_ref[...] = dwo_ref[...]
    share = LANES // ny
    mine = small_ref[...]
    shift = lax.rem(LANES - lax.rem(me, ny) * share, LANES)
    mine = pltpu.roll(mine, shift, 1)[:, :share]
    w_ref[...] = mine[:CONV]
    b_ref[...] = mine[CONV : CONV + 1]
    t_ref[...] = mine[5:6]
    s_ref[...] = mine[6:7]
    a_ref[...] = mine[CHUNKS:]


def body(
    ny,
    seq_in,
    gate_in,
    upstream,
    forget_flags,
    conv_weight,
    conv_bias,
    proj_weight,
    dt_weight,
    dt_bias,
    a_log,
    skip_gain,
):
    n_ctx, n_mp = lax.axis_size("ctx"), lax.axis_size("mp")
    nz = n_ctx // ny
    tokens, width = seq_in.shape
    tics, groups = tokens // CHUNKS, width // LANES
    rows, half, most = dt_weight.shape[0], width // 2, max(nz, ny)
    full, wide = (tokens, width), (tics, STATE, CHUNKS, LANES)
    line = (1, width)
    inputs = dict(
        seq=seq_in,
        gate=gate_in,
        up=upstream,
        flag=forget_flags.reshape(1, tokens),
        cw=conv_weight,
        cb=conv_bias.reshape(line),
        w=proj_weight,
        d=dt_weight,
        dbias=dt_bias.reshape(line),
        alog=a_log,
        skip=skip_gain.reshape(line),
    )
    outs = dict(
        grad=(full, F32),
        later=((CHUNKS, width), F32),
        mixo=(full, BF16),
        dwo=((rows, width), F32),
        smallo=((24, LANES), F32),
    )
    part = (n_mp, tokens // n_mp, PROJ)
    scratch = dict(
        x=(full, F32),
        g=(full, F32),
        gg=(full, F32),
        act=(full, F32),
        pre=(full, F32),
        step=(full, F32),
        sig=(full, F32),
        gas=(full, F32),
        actb=(full, BF16),
        half=(full, BF16),
        halo=((16, width), BF16),
        w_all=((nz, ny) + proj_weight.shape, BF16),
        d_all=((nz, ny) + dt_weight.shape, BF16),
        dt=((RANK, width), BF16),
        low_t=((RANK, tokens), BF16),
        p1=(part, BF16),
        q1=(part, BF16),
        acc1=(part[1:], BF16),
        proj=(part, BF16),
        p2=(part, BF16),
        q2=(part, BF16),
        acc2=(part[1:], BF16),
        gproj=(part, BF16),
        b=(wide, F32),
        c=(wide, F32),
        gb=(wide, F32),
        gc=(wide, F32),
        h=((tics + 1,) + wide[1:], F32),
        pe=((STATE, CHUNKS, width), F32),
        pq=((STATE, CHUNKS, width), F32),
        pack=((groups, 3 * STATE, LANES), BF16),
        ends=((2 * STATE, LANES), F32),
        rx=((ny, 3 * STATE, LANES), BF16),
        rowt=((3 * STATE, LANES), BF16),
        rz=((nz, 3 * STATE, LANES), BF16),
        backt=((ny, 2 * STATE, LANES), BF16),
        edges=((groups, 2 * STATE, LANES), BF16),
        fw=((ny, STATE, LANES), F32),
        bw=((ny, STATE, LANES), F32),
        mix=((tokens, LANES), F32),
        gpre=((tokens, LANES), F32),
        dw=((nz, ny, rows, width), BF16),
        ra=((most, most, rows, width), BF16),
        sa=((ny, rows, half), BF16),
        sb=((nz, rows, half), BF16),
        rra=((ny, rows, half), BF16),
        rrb=((nz, rows, half), BF16),
        sg=((groups, 24, LANES), F32),
        sr=((nz, 24, LANES), F32),
        ss=((24, LANES), F32),
        srr=((ny, 24, LANES), F32),
        head=((CHUNKS, width), F32),
    )
    names = list(inputs) + list(outs) + list(scratch) + ["send", "recv"]
    slots = 256
    grad, later, mix, dwo, small = call(
        functools.partial(mega_kernel, nz, ny, n_ctx, n_mp, names),
        list(outs.values()),
        list(inputs.values()),
        [pltpu.VMEM(s, d) for s, d in scratch.values()]
        + [pltpu.SemaphoreType.DMA((slots,)), pltpu.SemaphoreType.DMA((slots,))],
        1,
    )
    share = LANES // ny
    grad_seq, grad_gate, grad_dtw, g_w, g_b, g_t, g_a, g_s = call(
        functools.partial(end_kernel, n_ctx, ny),
        [
            (full, BF16),
            (full, BF16),
            ((rows, width), F32),
            ((CONV, share), F32),
            ((1, share), F32),
            ((1, share), F32),
            ((STATE, share), F32),
            ((1, share), F32),
        ],
        [grad, later, conv_weight, mix, dwo, small],
        [pltpu.VMEM(full, BF16)],
    )
    return (
        grad_seq,
        grad_gate,
        grad_dtw,
        g_w,
        g_b.reshape(share),
        g_t.reshape(share),
        g_a,
        g_s.reshape(share),
    )


def build(mesh, ny):
    return jax.shard_map(
        functools.partial(body, ny),
        mesh=mesh,
        in_specs=(
            P("ctx", "mp"),
            P("ctx", "mp"),
            P("ctx", "mp"),
            P("ctx"),
            P(None, "mp"),
            P("mp"),
            P(("mp", "ctx"), None),
            P("ctx", "mp"),
            P("mp"),
            P(None, "mp"),
            P("mp"),
        ),
        out_specs=(
            P("ctx", "mp"),
            P("ctx", "mp"),
            P("ctx", "mp"),
            P(None, ("mp", "ctx")),
            P(("mp", "ctx")),
            P(("mp", "ctx")),
            P(None, ("mp", "ctx")),
            P(("mp", "ctx")),
        ),
        check_vma=False,
    )


def solution(mesh):
    return build(mesh, NY)
```

```python
import functools

import jax
import jax.numpy as jnp
from jax import lax
from jax.experimental import pallas as pl
from jax.experimental.pallas import tpu as pltpu
from jax.sharding import PartitionSpec as P

STATE = 16
RANK = 512
CONV = 4
PROJ = RANK + 2 * STATE
LANES = 128
CHUNKS = 8
NY = 8
LOG2E = 1.4426950408889634
LN2 = 0.6931471805599453
SPLIT = 2
UNROLL_F = 2
UNROLL_B = 2
MESH = pl.DeviceIdType.MESH
F32, BF16 = jnp.float32, jnp.bfloat16
VMEM = pl.BlockSpec(memory_space=pltpu.VMEM)


def lanes_of(g):
    return pl.ds(pl.multiple_of(g * LANES, LANES), LANES)


def call(kernel, outs, args, scratch=(), collective=None):
    params = dict(vmem_limit_bytes=56 * 1024 * 1024)
    if collective is not None:
        params.update(collective_id=collective, has_side_effects=True)
    return pl.pallas_call(
        kernel,
        out_shape=tuple(jax.ShapeDtypeStruct(s, d) for s, d in outs),
        in_specs=[VMEM] * len(args),
        out_specs=tuple(VMEM for _ in outs),
        scratch_shapes=list(scratch),
        compiler_params=pltpu.CompilerParams(**params),
    )(*args)


def sigmoid(v):
    return 1.0 / (1.0 + jnp.exp(-v))


def split_total(total):
    high = total.astype(BF16)
    low = (total - high.astype(F32)).astype(BF16)
    shape = (CHUNKS, LANES)
    return jnp.concatenate(
        [jnp.broadcast_to(high.astype(F32), shape), jnp.broadcast_to(low.astype(F32), shape)], 0
    ).astype(BF16)


def permutation(tokens, transposed=False):
    row = lax.broadcasted_iota(jnp.int32, (tokens, tokens), 1 if transposed else 0)
    col = lax.broadcasted_iota(jnp.int32, (tokens, tokens), 0 if transposed else 1)
    tics = tokens // CHUNKS
    return jnp.where(col == (row & (CHUNKS - 1)) * tics + (row >> 3), 1.0, 0.0)


def dot(a, b, dims=((1,), (0,))):
    return lax.dot_general(a, b, (dims, ((), ())), preferred_element_type=F32)


def chunk_row():
    return lax.broadcasted_iota(jnp.int32, (1, CHUNKS, LANES), 1)


def with_earlier(x, edge, rim):
    last = pltpu.roll(x[x.shape[0] - rim :], 1, 1)
    last = jnp.where(chunk_row() == 0, edge[edge.shape[0] - rim :][:, None, :], last)
    return jnp.concatenate([last, x], axis=0)


def stacked(value):
    return value.reshape(value.shape[0] // CHUNKS, CHUNKS, LANES)


def flat(value):
    return value.reshape(-1, LANES)


class Net:
    def __init__(self, nz, ny, n_ctx, n_mp, send, recv):
        self.nz, self.ny, self.n_ctx, self.n_mp = nz, ny, n_ctx, n_mp
        self.send, self.recv = send, recv
        self.me, self.m = lax.axis_index("ctx"), lax.axis_index("mp")
        self.z, self.y = lax.div(self.me, ny), lax.rem(self.me, ny)
        self.slots, self.started = 0, []

    def y_of(self, k):
        return lax.rem(self.y + k + self.ny, self.ny)

    def z_of(self, k):
        return lax.rem(self.z + k + self.nz, self.nz)

    def m_of(self, k):
        return lax.rem(self.m + k, self.n_mp)

    def at_y(self, k):
        return (self.z * self.ny + self.y_of(k), self.m)

    def at_z(self, k):
        return (self.z_of(k) * self.ny + self.y, self.m)

    def at_m(self, k):
        return (self.me, self.m_of(k))

    def at_ctx(self, k):
        return (lax.rem(self.me + k + self.n_ctx, self.n_ctx), self.m)

    def greet(self):
        barrier = pltpu.get_barrier_semaphore()
        peers = [self.at_y(k) for k in range(1, self.ny)]
        peers += [self.at_z(k) for k in range(1, self.nz)]
        peers += [self.at_m(k) for k in range(1, self.n_mp)]
        peers += [self.at_ctx(1), self.at_ctx(-1)]
        for peer in peers:
            pl.semaphore_signal(barrier, inc=1, device_id=peer, device_id_type=MESH)
        return lambda: pl.semaphore_wait(barrier, len(peers))

    def take(self, count):
        first = self.slots
        self.slots += count
        return first

    def copy(self, src, dst, slot, peer):
        return pltpu.make_async_remote_copy(
            src_ref=src,
            dst_ref=dst,
            send_sem=self.send.at[slot],
            recv_sem=self.recv.at[slot],
            device_id=peer,
            device_id_type=MESH,
        )

    def go(self, src, dst, peer):
        made = self.copy(src, dst, self.take(1), peer)
        made.start()
        self.started.append(made)
        return made

    def finish(self):
        for made in self.started:
            made.wait_send()


def arrived(copies):
    for made in copies:
        made.wait_recv()


def ring_start(net, size, place, peer, part):
    if size != 8:
        return [net.go(part(place(0), 2), part(place(0), 2), peer(k)) for k in range(1, size)]
    return [net.go(part(place(0), 2), part(place(0), 2), peer(k)) for k in (2, -2, 1, -1)]


def ring_relay(net, size, place, peer, part, first):
    if size != 8:
        arrived(first)
        return []
    arrived(first[:2])
    made = [
        net.go(part(place(-2), 0), part(place(-2), 0), peer(2)),
        net.go(part(place(2), 1), part(place(2), 1), peer(-2)),
        net.go(part(place(-2), 2), part(place(-2), 2), peer(1)),
        net.go(part(place(2), 2), part(place(2), 2), peer(-1)),
    ]
    return made


def cut(ref, size, axis, lanes):
    def part(origin, which):
        span = pl.ds(0, size) if which == 2 else pl.ds(which * (size // 2), size // 2)
        if axis == "z":
            return ref.at[origin, span, :, lanes]
        return ref.at[span, origin, :, lanes]

    return part


def mega_kernel(nz, ny, n_ctx, n_mp, names, *refs):
    r = dict(zip(names, refs))
    net = Net(nz, ny, n_ctx, n_mp, r["send"], r["recv"])
    z, y, m = net.z, net.y, net.m
    seq_ref, alog_ref, skip_ref = r["seq"], r["alog"], r["skip"]
    tokens, width = seq_ref.shape
    tics, groups = tokens // CHUNKS, width // LANES
    half_width = width // 2
    row = chunk_row()
    g_ref, gg_ref, x_ref = r["g"], r["gg"], r["x"]
    wo_ref, do_ref = r["w_all"], r["d_all"]
    net.greet()()

    w_cut = 2 * LANES
    w_lo, w_hi = pl.ds(0, w_cut), pl.ds(w_cut, PROJ - w_cut)
    d_lo, d_hi = pl.ds(0, half_width), pl.ds(half_width, half_width)

    def first_leg(src, ref, lo, hi):
        a = [net.go(src.at[:, lo], ref.at[z, y, :, lo], net.at_y(k)) for k in range(1, ny)]
        b = [net.go(src.at[:, hi], ref.at[z, y, :, hi], net.at_z(k)) for k in range(1, nz)]
        return a, b

    w_a, w_b = first_leg(r["w"], wo_ref, w_lo, w_hi)
    halo = net.go(seq_ref.at[pl.ds(tokens - 16, 16)], r["halo"], net.at_ctx(1))
    perm = permutation(tokens)
    signed = (perm * -r["flag"][...].astype(F32)).astype(BF16)
    perm = perm.astype(BF16)
    x_ref[...] = dot(perm, seq_ref[...])
    g_ref[...] = dot(perm, r["gate"][...])
    gg_ref[...] = dot(signed, r["up"][...])
    wo_ref[z, y] = r["w"][...]
    do_ref[z, y] = r["d"][...]
    def legs(ref, lo, hi):
        return (
            (nz, net.z_of, net.at_z, cut(ref, ny, "z", lo)),
            (ny, net.y_of, net.at_y, cut(ref, nz, "y", hi)),
        )

    w_za, w_yb = legs(wo_ref, w_lo, w_hi)
    arrived(w_a)
    w_a = ring_start(net, *w_za)
    arrived(w_b)
    w_b = ring_start(net, *w_yb)
    d_a, d_b = first_leg(r["d"], do_ref, d_lo, d_hi)
    halo.wait_recv()
    first_block = net.me == 0
    act_ref, pre_ref, actb_ref = r["act"], r["pre"], r["actb"]

    def conv(g, carry):
        at = lanes_of(g)
        x = stacked(x_ref[:, at])
        edge = jnp.where(first_block, 0.0, r["halo"][:, at].astype(F32))
        padded = with_earlier(x, edge, CONV - 1)
        taps = r["cw"][:, at]
        pre = r["cb"][:, at][None] + taps[0:1][None] * padded[: x.shape[0]]
        for k in range(1, CONV):
            pre = pre + taps[k : k + 1][None] * padded[k : k + x.shape[0]]
        pre = flat(pre)
        act = (pre * sigmoid(pre)).astype(BF16)
        pre_ref[:, at] = pre
        actb_ref[:, at] = act
        act_ref[:, at] = act.astype(F32)
        return carry

    def gates(g, carry):
        at = lanes_of(g)
        gate = g_ref[:, at]
        out = gg_ref[:, at]
        s = sigmoid(gate)
        g_ref[:, at] = out * (gate * s)
        gg_ref[:, at] = out * (s * (1.0 + gate * (1.0 - s)))
        return carry

    lax.fori_loop(0, groups, conv, 0)
    lax.fori_loop(0, groups, gates, 0)
    w_a2 = ring_relay(net, *w_za, w_a)
    w_b2 = ring_relay(net, *w_yb, w_b)
    d_za, d_yb = legs(do_ref, d_lo, d_hi)
    arrived(d_a)
    d_a = ring_start(net, *d_za)
    arrived(d_b)
    d_b = ring_start(net, *d_yb)
    if nz == 8:
        arrived(w_a[2:])
    if ny == 8:
        arrived(w_b[2:])
    arrived(w_a2 + w_b2)

    sum_shape = (n_mp, tokens // n_mp, PROJ)
    w_full = wo_ref[...].reshape(width, PROJ)
    r["p1"][...] = dot(actb_ref[...], w_full).astype(BF16).reshape(sum_shape)

    def sum_start(p_ref, r_ref):
        return [net.go(p_ref.at[net.m_of(k)], r_ref.at[k], net.at_m(k)) for k in range(1, n_mp)]

    def sum_turn(first, p_ref, r_ref, acc_ref, o_ref):
        total = p_ref[m].astype(F32)
        for k in range(1, n_mp):
            first[k - 1].wait_recv()
            total = total + r_ref[k].astype(F32)
        acc_ref[...] = total.astype(BF16)
        o_ref[m] = acc_ref[...]
        return [net.go(acc_ref, o_ref.at[m], net.at_m(k)) for k in range(1, n_mp)]

    s1 = sum_start(r["p1"], r["q1"])
    d_a2 = ring_relay(net, *d_za, d_a)
    d_b2 = ring_relay(net, *d_yb, d_b)
    s2 = sum_turn(s1, r["p1"], r["q1"], r["acc1"], r["proj"])
    if nz == 8:
        arrived(d_a[2:])
    if ny == 8:
        arrived(d_b[2:])
    arrived(d_a2 + d_b2)

    def lay_out(i, carry):
        rows = do_ref.shape[2] * ny
        block = do_ref[i].astype(F32).reshape(rows, width)
        r["dt"][pl.ds(pl.multiple_of(i * rows, rows), rows)] = block.astype(BF16)
        return carry

    lax.fori_loop(0, nz, lay_out, 0)
    dt_ref = r["dt"]
    arrived(s2)

    proj = r["proj"][...].reshape(tokens, PROJ)
    low = proj[:, :RANK]
    cols = proj[:, RANK:].astype(F32)
    r["low_t"][...] = low.astype(F32).T.astype(BF16)
    step_ref, sig_ref = r["step"], r["sig"]
    step_ref[...] = dot(low, dt_ref[...])
    b_ref, c_ref = r["b"], r["c"]

    def spread(first, out_ref):
        for n in range(STATE):
            col = cols[:, first + n : first + n + 1]
            out_ref[:, n] = stacked(jnp.broadcast_to(col, (tokens, LANES)))

    spread(0, b_ref)
    spread(STATE, c_ref)
    rx_ref, row_ref, rz_ref, back_ref, edge_ref = r["rx"], r["rowt"], r["rz"], r["backt"], r["edges"]
    pe_ref, pq_ref, pack_ref, ends_ref = r["pe"], r["pq"], r["pack"], r["ends"]
    wide = (STATE, CHUNKS, LANES)
    base1 = net.take(ny)

    def pack_copy(k):
        peer = (z * ny + lax.rem(y + k, ny), m)
        return net.copy(pack_ref.at[lax.rem(y + k, ny)], rx_ref.at[y], base1 + k, peer)

    def here_of(t):
        return pl.ds(pl.multiple_of(t * CHUNKS, CHUNKS), CHUNKS)

    def local(i, carry):
        k = lax.rem(i + 1, ny)
        g = lax.rem(y + k, ny)
        at = lanes_of(g)
        pre = step_ref[:, at] + r["dbias"][:, at]
        step_ref[:, at] = jnp.maximum(pre, 0.0) + jnp.log1p(jnp.exp(-jnp.abs(pre)))
        sig_ref[:, at] = sigmoid(pre)
        a2 = jnp.broadcast_to((-LOG2E * jnp.exp(alog_ref[:, at]))[:, None, :], wide)

        def ahead(t, carry):
            state, total = carry
            here = here_of(t)
            step = step_ref[here, at]
            flow = step * act_ref[here, at]
            state = jnp.exp2(step[None] * a2) * state + b_ref[t] * flow[None]
            return state, total + step

        zero = jnp.zeros(wide, F32)
        state, total = lax.fori_loop(
            0, tics, ahead, (zero, jnp.zeros((CHUNKS, LANES), F32)), unroll=4
        )

        def back(i, adjoint):
            t = tics - 1 - i
            here = here_of(t)
            step = step_ref[here, at]
            return jnp.exp2(step[None] * a2) * (c_ref[t] * g_ref[here, at][None] + adjoint)

        adjoint = lax.fori_loop(0, tics, back, zero, unroll=4)
        left = jnp.exp2(total[None] * a2)
        right = left
        shift = 1
        while shift < CHUNKS:
            in_left = row >= shift
            in_right = row < CHUNKS - shift
            state = state + left * jnp.where(in_left, pltpu.roll(state, shift, 1), 0.0)
            left = left * jnp.where(in_left, pltpu.roll(left, shift, 1), 1.0)
            adjoint = adjoint + right * jnp.where(
                in_right, pltpu.roll(adjoint, CHUNKS - shift, 1), 0.0
            )
            right = right * jnp.where(in_right, pltpu.roll(right, CHUNKS - shift, 1), 1.0)
            shift *= 2
        pe_ref[:, :, at] = state
        pq_ref[:, :, at] = adjoint
        for n in range(STATE):
            ends_ref[pl.ds(n, 1)] = state[n, CHUNKS - 1 : CHUNKS]
            ends_ref[pl.ds(STATE + n, 1)] = adjoint[n, 0:1]
        pack_ref[g, pl.ds(0, 2 * STATE)] = ends_ref[...].astype(BF16)
        pack_ref[g, pl.ds(2 * STATE, STATE)] = split_total(jnp.sum(total, axis=0, keepdims=True))

        @pl.when(i < ny - 1)
        def _():
            pack_copy(k).start()

        return carry

    lax.fori_loop(0, groups, local, 0)

    fw_ref, bw_ref = r["fw"], r["bw"]
    rx_ref[y] = pack_ref[y]
    my_a2 = -LOG2E * jnp.exp(alog_ref[:, lanes_of(y)])
    gb_ref, gc_ref = r["gb"], r["gc"]
    gb_ref[...] = jnp.zeros(gb_ref.shape, F32)
    gc_ref[...] = jnp.zeros(gc_ref.shape, F32)
    arrived([pack_copy(k) for k in range(1, ny)])

    def total_of(block):
        tail = block[2 * STATE :].astype(F32)
        return tail[0:1] + tail[CHUNKS : CHUNKS + 1]

    zero = jnp.zeros((STATE, LANES), F32)
    totals = [total_of(rx_ref[j]) for j in range(ny)]
    forward, sums = zero, jnp.zeros((1, LANES), F32)
    before, behind = [], [None] * ny
    for j in range(ny):
        fw_ref[j] = forward
        before.append(sums)
        forward = jnp.exp2(my_a2 * totals[j]) * forward + rx_ref[j, pl.ds(0, STATE)].astype(F32)
        sums = sums + totals[j]
    backward, tail_sum = zero, jnp.zeros((1, LANES), F32)
    for j in reversed(range(ny)):
        bw_ref[j] = backward
        behind[j] = tail_sum
        backward = jnp.exp2(my_a2 * totals[j]) * backward + rx_ref[j, pl.ds(STATE, STATE)].astype(F32)
        tail_sum = tail_sum + totals[j]
    row_ref[pl.ds(0, STATE)] = forward.astype(BF16)
    row_ref[pl.ds(STATE, STATE)] = backward.astype(BF16)
    row_ref[pl.ds(2 * STATE, STATE)] = split_total(sums)
    c2 = [net.go(row_ref, rz_ref.at[z], net.at_z(k)) for k in range(1, nz)]
    rz_ref[z] = row_ref[...]
    arrived(c2)
    head, tail = zero, zero
    for k in range(nz):
        block = rz_ref[k]
        fresh = jnp.exp2(my_a2 * total_of(block)) * head + block[:STATE].astype(F32)
        head = jnp.where(k < z, fresh, head)
    for k in reversed(range(nz)):
        block = rz_ref[k]
        fresh = jnp.exp2(my_a2 * total_of(block)) * tail + block[STATE : 2 * STATE].astype(F32)
        tail = jnp.where(k > z, fresh, tail)
    for j in range(ny):
        into = fw_ref[j] + jnp.exp2(my_a2 * before[j]) * head
        outof = bw_ref[j] + jnp.exp2(my_a2 * behind[j]) * tail
        back_ref[j, pl.ds(0, STATE)] = into.astype(BF16)
        back_ref[j, pl.ds(STATE, STATE)] = outof.astype(BF16)
    base3 = net.take(ny)

    def edge_copy(k):
        peer = (z * ny + lax.rem(y + k, ny), m)
        return net.copy(back_ref.at[lax.rem(y + k, ny)], edge_ref.at[y], base3 + k, peer)

    edge_ref[y] = back_ref[y]
    for k in range(1, ny):
        edge_copy(k).start()

    h_ref, mix_ref, gpre_ref, half_ref = r["h"], r["mix"], r["gpre"], r["half"]
    gas_ref, dw_ref, ra_ref, sg_ref = r["gas"], r["dw"], r["ra"], r["sg"]
    flow_ref, slope_ref = r["flow"], r["slope"]
    pairs = groups // 2
    base = net.take(pairs * 8)

    def dw_copy(p, k, along_z):
        at = pl.ds(pl.multiple_of(p * 2 * LANES, 2 * LANES), 2 * LANES)
        if along_z:
            src, peer = dw_ref.at[net.z_of(k), :, :, at], net.at_z(k)
        else:
            src, peer = dw_ref.at[:, net.y_of(k), :, at], net.at_y(k)
        return net.copy(src, ra_ref.at[k, :, :, at], base + p * 8 + k, peer)

    def main(g):
        at = lanes_of(g)

        @pl.when(g != y)
        def _():
            edge_copy(lax.rem(y - g + ny, ny)).wait_recv()

        a2 = jnp.broadcast_to((-LOG2E * jnp.exp(alog_ref[:, at]))[:, None, :], wide)
        skip = skip_ref[:, at]
        total = jnp.sum(stacked(step_ref[:, at]), axis=0)[None]
        left, right = total, total
        shift = 1
        while shift < CHUNKS:
            left = left + jnp.where(row >= shift, pltpu.roll(left, shift, 1), 0.0)
            right = right + jnp.where(
                row < CHUNKS - shift, pltpu.roll(right, CHUNKS - shift, 1), 0.0
            )
            shift *= 2
        ends = edge_ref[g].astype(F32)
        into = jnp.broadcast_to(ends[:STATE][:, None, :], wide)
        outof = jnp.broadcast_to(ends[STATE:][:, None, :], wide)
        state = jnp.where(row >= 1, pltpu.roll(pe_ref[:, :, at], 1, 1), 0.0)
        state = state + jnp.exp2(a2 * (left - total)) * into
        adjoint = jnp.where(row < CHUNKS - 1, pltpu.roll(pq_ref[:, :, at], CHUNKS - 1, 1), 0.0)
        adjoint = adjoint + jnp.exp2(a2 * (right - total)) * outof
        h_ref[0] = state

        def ahead(t, state):
            here = here_of(t)
            step = step_ref[here, at]
            act = act_ref[here, at]
            state = jnp.exp2(step[None] * a2) * state + b_ref[t] * (step * act)[None]
            h_ref[t + 1] = state
            mixed = jnp.sum(c_ref[t] * state, axis=0) + skip * act
            mix_ref[here] = mixed * gg_ref[here, at]
            return state

        lax.fori_loop(0, tics, ahead, state, unroll=UNROLL_F)
        r["mixo"][:, at] = mix_ref[...].astype(BF16)
        none = jnp.zeros((CHUNKS, LANES), F32)
        pre_sum, skip_sum = none, none
        span = STATE // SPLIT
        for part in range(SPLIT):
            of = slice(part * span, part * span + span)
            ns = pl.ds(part * span, span)
            a2_part = a2[of]
            opening, closing = part == 0, part == SPLIT - 1

            def back(i, carry):
                adjoint, rate_sum, pre_sum, skip_sum = carry
                t = tics - 1 - i
                here = here_of(t)
                step = step_ref[here, at]
                act = act_ref[here, at]
                grad = g_ref[here, at]
                lam = c_ref[t, ns] * grad[None] + adjoint
                adjoint = jnp.exp2(step[None] * a2_part) * lam
                pull = adjoint * h_ref[t, ns]
                gc_ref[t, ns] += h_ref[t + 1, ns] * grad[None]
                gb_ref[t, ns] += lam * (step * act)[None]
                slopes = pull * a2_part
                flow = jnp.sum(lam * b_ref[t, ns], axis=0)
                slope = jnp.sum(slopes, axis=0)
                if not opening:
                    flow = flow + flow_ref[here]
                    slope = slope + slope_ref[here]
                if closing:
                    gas_ref[here, at] = flow * step + skip * grad
                    pre = (flow * act + slope * LN2) * sig_ref[here, at]
                    gpre_ref[here] = pre
                    pre_sum = pre_sum + pre
                    skip_sum = skip_sum + grad * act
                else:
                    flow_ref[here] = flow
                    slope_ref[here] = slope
                return (adjoint, rate_sum + slopes * step[None], pre_sum, skip_sum)

            _, rate_sum, pre_sum, skip_sum = lax.fori_loop(
                0,
                tics,
                back,
                (adjoint[of], jnp.zeros((span, CHUNKS, LANES), F32), pre_sum, skip_sum),
                unroll=UNROLL_B,
            )
            for n in range(span):
                sg_ref[g, pl.ds(CHUNKS + part * span + n, 1)] = LN2 * jnp.sum(
                    rate_sum[n], axis=0, keepdims=True
                )
        half_ref[:, at] = gpre_ref[...].astype(BF16)
        sg_ref[g, pl.ds(0, 1)] = jnp.sum(pre_sum, axis=0, keepdims=True)
        sg_ref[g, pl.ds(1, 1)] = jnp.sum(skip_sum, axis=0, keepdims=True)
        sg_ref[g, pl.ds(2, CHUNKS - 2)] = jnp.zeros((CHUNKS - 2, LANES), F32)

    def main_pair(i, carry):
        turn = lax.rem(i, 2) * (pairs // 2) + lax.div(i, 2)
        p = lax.rem(lax.div(y, 2) + turn, pairs)

        def one(j, carry):
            main(2 * p + lax.rem(y + j, 2))
            return carry

        lax.fori_loop(0, 2, one, 0)
        at = pl.ds(pl.multiple_of(p * 2 * LANES, 2 * LANES), 2 * LANES)
        dw_ref[:, :, :, at] = (
            dot(r["low_t"][...], half_ref[:, at])
            .reshape(dw_ref.shape[:3] + (2 * LANES,))
            .astype(BF16)
        )

        @pl.when(p < pairs // 2)
        def _():
            for k in range(1, nz):
                dw_copy(p, k, True).start()

        @pl.when(p >= pairs // 2)
        def _():
            for k in range(1, ny):
                dw_copy(p, k, False).start()

        return carry

    lax.fori_loop(0, pairs, main_pair, 0)

    pick = jnp.where(
        lax.broadcasted_iota(jnp.int32, (STATE * LANES, STATE), 0) // LANES
        == lax.broadcasted_iota(jnp.int32, (STATE * LANES, STATE), 1),
        1.0,
        0.0,
    ).astype(BF16)

    def folded(ref):
        side = jnp.concatenate([flat(ref[:, n]) for n in range(STATE)], axis=1)
        return dot(side.astype(BF16), pick)

    r["p2"][:, :, pl.ds(0, RANK)] = (
        dot(half_ref[...], dt_ref[...], ((1,), (1,))).astype(BF16).reshape(sum_shape[:2] + (RANK,))
    )
    r["p2"][:, :, pl.ds(RANK, 2 * STATE)] = (
        jnp.concatenate([folded(gb_ref), folded(gc_ref)], axis=1)
        .astype(BF16)
        .reshape(sum_shape[:2] + (2 * STATE,))
    )
    s3 = sum_start(r["p2"], r["q2"])
    t1 = [net.go(sg_ref.at[net.z_of(k)], r["sr"].at[k], net.at_z(k)) for k in range(1, nz)]
    sa_ref, sb_ref, rra_ref, rrb_ref = r["sa"], r["sb"], r["rra"], r["rrb"]
    lo, hi = pl.ds(0, half_width), pl.ds(half_width, half_width)

    def add_a(i, carry):
        total = dw_ref[z, i, :, lo].astype(F32)
        for k in range(1, nz):
            total = total + ra_ref[k, i, :, lo].astype(F32)
        sa_ref[i] = total.astype(BF16)
        return carry

    def add_b(i, carry):
        total = dw_ref[i, y, :, hi].astype(F32)
        for k in range(1, ny):
            total = total + ra_ref[k, i, :, hi].astype(F32)
        sb_ref[i] = total.astype(BF16)
        return carry

    s4 = sum_turn(s3, r["p2"], r["q2"], r["acc2"], r["gproj"])
    arrived([dw_copy(p, k, True) for p in range(pairs // 2) for k in range(1, nz)])
    lax.fori_loop(0, ny, add_a, 0)
    a2nd = [net.go(sa_ref.at[net.y_of(k)], rra_ref.at[k], net.at_y(k)) for k in range(1, ny)]
    arrived([dw_copy(p, k, False) for p in range(pairs // 2, pairs) for k in range(1, ny)])
    lax.fori_loop(0, nz, add_b, 0)
    b2nd = [net.go(sb_ref.at[net.z_of(k)], rrb_ref.at[k], net.at_z(k)) for k in range(1, nz)]
    arrived(t1)
    total = sg_ref[z]
    for k in range(1, nz):
        total = total + r["sr"][k]
    r["ss"][...] = total
    t2 = [net.go(r["ss"], r["srr"].at[k], net.at_y(k)) for k in range(1, ny)]
    arrived(s4)

    out_ref, head_ref, cg_ref = r["grad"], r["head"], r["cg"]
    out_ref[...] = dot(r["gproj"][...].reshape(tokens, PROJ), wo_ref[...].reshape(width, PROJ), ((1,), (1,)))

    def close(g, carry):
        at = lanes_of(g)
        pre = pre_ref[:, at]
        s = sigmoid(pre)
        grad = (gas_ref[:, at] + out_ref[:, at]) * (s * (1.0 + pre * (1.0 - s)))
        out_ref[:, at] = grad
        grad = stacked(grad)
        edge = jnp.where(first_block, 0.0, r["halo"][:, at].astype(F32))
        x = stacked(x_ref[:, at])
        padded = with_earlier(x, edge, CONV - 1)
        for k in range(CONV):
            part = jnp.sum(grad * padded[k : k + x.shape[0]], axis=0)
            cg_ref[g, pl.ds(k, 1)] = jnp.sum(part, axis=0, keepdims=True)
        cg_ref[g, pl.ds(CONV, 1)] = jnp.sum(jnp.sum(grad, axis=0), axis=0, keepdims=True)
        cg_ref[g, pl.ds(CONV + 1, 3)] = jnp.zeros((3, LANES), F32)
        head_ref[:, at] = jnp.zeros((CHUNKS, LANES), F32)
        for k in range(CONV - 1):
            head_ref[pl.ds(k, 1), at] = grad[k, 0:1]
        return carry

    lax.fori_loop(0, groups, close, 0)
    later = net.go(head_ref, r["later"], net.at_ctx(-1))
    u1 = [net.go(cg_ref.at[net.z_of(k)], r["cr"].at[k], net.at_z(k)) for k in range(1, nz)]
    arrived(a2nd)
    total = sa_ref[y].astype(F32)
    for k in range(1, ny):
        total = total + rra_ref[k].astype(F32)
    r["dwo"][:, lo] = total
    arrived(b2nd)
    total = sb_ref[z].astype(F32)
    for k in range(1, nz):
        total = total + rrb_ref[k].astype(F32)
    r["dwo"][:, hi] = total
    arrived(t2)
    total = r["ss"][...]
    for k in range(1, ny):
        total = total + r["srr"][k]
    r["smallo"][pl.ds(CHUNKS, 24)] = total
    arrived(u1)
    total = cg_ref[z]
    for k in range(1, nz):
        total = total + r["cr"][k]
    r["cs"][...] = total
    u2 = [net.go(r["cs"], r["crr"].at[k], net.at_y(k)) for k in range(1, ny)]
    later.wait_recv()
    last_block = net.me == n_ctx - 1

    def conv_back(g, carry):
        at = lanes_of(g)
        grad = stacked(out_ref[:, at])
        edge = jnp.where(last_block, 0.0, r["later"][:, at])
        rest = pltpu.roll(grad[: CONV - 1], CHUNKS - 1, 1)
        rest = jnp.where(row == CHUNKS - 1, edge[: CONV - 1][:, None, :], rest)
        padded = jnp.concatenate([grad, rest], axis=0)
        taps = r["cw"][:, at]
        total = taps[CONV - 1 :][None] * grad
        for k in range(CONV - 1):
            off = CONV - 1 - k
            total = total + taps[k : k + 1][None] * padded[off : off + grad.shape[0]]
        r["seqo"][:, at] = flat(total).astype(BF16)
        return carry

    lax.fori_loop(0, groups, conv_back, 0)
    for k in range(1, ny):
        pack_copy(k).wait_send()
        edge_copy(k).wait_send()
    for p in range(pairs):
        along_z = p < pairs // 2
        for k in range(1, nz if along_z else ny):
            dw_copy(p, k, along_z).wait_send()
    arrived(u2)
    total = r["cs"][...]
    for k in range(1, ny):
        total = total + r["crr"][k]
    r["smallo"][pl.ds(0, CHUNKS)] = total
    net.finish()


def end_kernel(
    ny,
    seq_ref,
    mix_ref,
    dwo_ref,
    small_ref,
    out_ref,
    gate_ref,
    dw_ref,
    w_ref,
    b_ref,
    t_ref,
    a_ref,
    s_ref,
):
    tokens, width = seq_ref.shape
    me = lax.axis_index("ctx")
    unperm = permutation(tokens, True).astype(BF16)
    out_ref[...] = dot(unperm, seq_ref[...]).astype(BF16)
    gate_ref[...] = dot(unperm, mix_ref[...]).astype(BF16)
    dw_ref[...] = dwo_ref[...]
    share = LANES // ny
    shift = lax.rem(LANES - lax.rem(me, ny) * share, LANES)
    mine = pltpu.roll(small_ref[...], shift, 1)[:, :share]
    w_ref[...] = mine[:CONV]
    b_ref[...] = mine[CONV : CONV + 1]
    t_ref[...] = mine[CHUNKS : CHUNKS + 1]
    s_ref[...] = mine[CHUNKS + 1 : CHUNKS + 2]
    a_ref[...] = mine[2 * CHUNKS :]


def body(
    ny,
    seq_in,
    gate_in,
    upstream,
    forget_flags,
    conv_weight,
    conv_bias,
    proj_weight,
    dt_weight,
    dt_bias,
    a_log,
    skip_gain,
):
    n_ctx, n_mp = lax.axis_size("ctx"), lax.axis_size("mp")
    nz = n_ctx // ny
    tokens, width = seq_in.shape
    tics, groups = tokens // CHUNKS, width // LANES
    rows, half, most = dt_weight.shape[0], width // 2, max(nz, ny)
    full, wide = (tokens, width), (tics, STATE, CHUNKS, LANES)
    line = (1, width)
    inputs = dict(
        seq=seq_in,
        gate=gate_in,
        up=upstream,
        flag=forget_flags.reshape(1, tokens),
        cw=conv_weight,
        cb=conv_bias.reshape(line),
        w=proj_weight,
        d=dt_weight,
        dbias=dt_bias.reshape(line),
        alog=a_log,
        skip=skip_gain.reshape(line),
    )
    outs = dict(
        seqo=(full, BF16),
        mixo=(full, BF16),
        dwo=((rows, width), F32),
        smallo=((24 + CHUNKS, LANES), F32),
    )
    part = (n_mp, tokens // n_mp, PROJ)
    scratch = dict(
        x=(full, F32),
        g=(full, F32),
        gg=(full, F32),
        act=(full, F32),
        pre=(full, F32),
        step=(full, F32),
        sig=(full, F32),
        gas=(full, F32),
        actb=(full, BF16),
        half=(full, BF16),
        halo=((16, width), BF16),
        w_all=((nz, ny) + proj_weight.shape, BF16),
        d_all=((nz, ny) + dt_weight.shape, BF16),
        dt=((RANK, width), BF16),
        low_t=((RANK, tokens), BF16),
        p1=(part, BF16),
        q1=(part, BF16),
        acc1=(part[1:], BF16),
        proj=(part, BF16),
        p2=(part, BF16),
        q2=(part, BF16),
        acc2=(part[1:], BF16),
        gproj=(part, BF16),
        b=(wide, F32),
        c=(wide, F32),
        gb=(wide, F32),
        gc=(wide, F32),
        h=((tics + 1,) + wide[1:], F32),
        pe=((STATE, CHUNKS, width), F32),
        pq=((STATE, CHUNKS, width), F32),
        pack=((groups, 3 * STATE, LANES), BF16),
        ends=((2 * STATE, LANES), F32),
        rx=((ny, 3 * STATE, LANES), BF16),
        rowt=((3 * STATE, LANES), BF16),
        rz=((nz, 3 * STATE, LANES), BF16),
        backt=((ny, 2 * STATE, LANES), BF16),
        edges=((groups, 2 * STATE, LANES), BF16),
        fw=((ny, STATE, LANES), F32),
        bw=((ny, STATE, LANES), F32),
        mix=((tokens, LANES), F32),
        gpre=((tokens, LANES), F32),
        dw=((nz, ny, rows, width), BF16),
        ra=((most, most, rows, width), BF16),
        sa=((ny, rows, half), BF16),
        sb=((nz, rows, half), BF16),
        rra=((ny, rows, half), BF16),
        rrb=((nz, rows, half), BF16),
        sg=((groups, 24, LANES), F32),
        sr=((nz, 24, LANES), F32),
        ss=((24, LANES), F32),
        srr=((ny, 24, LANES), F32),
        head=((CHUNKS, width), F32),
        later=((CHUNKS, width), F32),
        grad=(full, F32),
        flow=((tokens, LANES), F32),
        slope=((tokens, LANES), F32),
        cg=((groups, CHUNKS, LANES), F32),
        cr=((nz, CHUNKS, LANES), F32),
        cs=((CHUNKS, LANES), F32),
        crr=((ny, CHUNKS, LANES), F32),
    )
    names = list(inputs) + list(outs) + list(scratch) + ["send", "recv"]
    slots = 256
    seq, mix, dwo, small = call(
        functools.partial(mega_kernel, nz, ny, n_ctx, n_mp, names),
        list(outs.values()),
        list(inputs.values()),
        [pltpu.VMEM(s, d) for s, d in scratch.values()]
        + [pltpu.SemaphoreType.DMA((slots,)), pltpu.SemaphoreType.DMA((slots,))],
        1,
    )
    share = LANES // ny
    grad_seq, grad_gate, grad_dtw, g_w, g_b, g_t, g_a, g_s = call(
        functools.partial(end_kernel, ny),
        [
            (full, BF16),
            (full, BF16),
            ((rows, width), F32),
            ((CONV, share), F32),
            ((1, share), F32),
            ((1, share), F32),
            ((STATE, share), F32),
            ((1, share), F32),
        ],
        [seq, mix, dwo, small],
    )
    return (
        grad_seq,
        grad_gate,
        grad_dtw,
        g_w,
        g_b.reshape(share),
        g_t.reshape(share),
        g_a,
        g_s.reshape(share),
    )


def build(mesh, ny):
    return jax.shard_map(
        functools.partial(body, ny),
        mesh=mesh,
        in_specs=(
            P("ctx", "mp"),
            P("ctx", "mp"),
            P("ctx", "mp"),
            P("ctx"),
            P(None, "mp"),
            P("mp"),
            P(("mp", "ctx"), None),
            P("ctx", "mp"),
            P("mp"),
            P(None, "mp"),
            P("mp"),
        ),
        out_specs=(
            P("ctx", "mp"),
            P("ctx", "mp"),
            P("ctx", "mp"),
            P(None, ("mp", "ctx")),
            P(("mp", "ctx")),
            P(("mp", "ctx")),
            P(None, ("mp", "ctx")),
            P(("mp", "ctx")),
        ),
        check_vma=False,
    )


def solution(mesh):
    return build(mesh, NY)
```

```python
import functools

import jax
import jax.numpy as jnp
from jax import lax
from jax.experimental import pallas as pl
from jax.experimental.pallas import tpu as pltpu
from jax.sharding import PartitionSpec as P

STATE = 16
RANK = 512
CONV = 4
PROJ = RANK + 2 * STATE
LANES = 128
CHUNKS = 8
NY = 8
LOG2E = 1.4426950408889634
LN2 = 0.6931471805599453
SPLIT = 2
UNROLL_F = 4
UNROLL_B = 4
UNROLL_L = 4
MESH = pl.DeviceIdType.MESH
F32, BF16 = jnp.float32, jnp.bfloat16
VMEM = pl.BlockSpec(memory_space=pltpu.VMEM)


def lanes_of(g):
    return pl.ds(pl.multiple_of(g * LANES, LANES), LANES)


def call(kernel, outs, args, scratch=(), collective=None):
    params = dict(vmem_limit_bytes=56 * 1024 * 1024)
    if collective is not None:
        params.update(collective_id=collective, has_side_effects=True)
    return pl.pallas_call(
        kernel,
        out_shape=tuple(jax.ShapeDtypeStruct(s, d) for s, d in outs),
        in_specs=[VMEM] * len(args),
        out_specs=tuple(VMEM for _ in outs),
        scratch_shapes=list(scratch),
        compiler_params=pltpu.CompilerParams(**params),
    )(*args)


def sigmoid(v):
    return 1.0 / (1.0 + jnp.exp(-v))


def split_total(total):
    high = total.astype(BF16)
    low = (total - high.astype(F32)).astype(BF16)
    shape = (CHUNKS, LANES)
    return jnp.concatenate(
        [jnp.broadcast_to(high.astype(F32), shape), jnp.broadcast_to(low.astype(F32), shape)], 0
    ).astype(BF16)


def permutation(tokens, transposed=False):
    row = lax.broadcasted_iota(jnp.int32, (tokens, tokens), 1 if transposed else 0)
    col = lax.broadcasted_iota(jnp.int32, (tokens, tokens), 0 if transposed else 1)
    tics = tokens // CHUNKS
    return jnp.where(col == (row & (CHUNKS - 1)) * tics + (row >> 3), 1.0, 0.0)


def dot(a, b, dims=((1,), (0,))):
    return lax.dot_general(a, b, (dims, ((), ())), preferred_element_type=F32)


def chunk_row():
    return lax.broadcasted_iota(jnp.int32, (1, CHUNKS, LANES), 1)


def with_earlier(x, edge, rim):
    last = pltpu.roll(x[x.shape[0] - rim :], 1, 1)
    last = jnp.where(chunk_row() == 0, edge[edge.shape[0] - rim :][:, None, :], last)
    return jnp.concatenate([last, x], axis=0)


def stacked(value):
    return value.reshape(value.shape[0] // CHUNKS, CHUNKS, LANES)


def flat(value):
    return value.reshape(-1, LANES)


class Net:
    def __init__(self, nz, ny, n_ctx, n_mp, send, recv):
        self.nz, self.ny, self.n_ctx, self.n_mp = nz, ny, n_ctx, n_mp
        self.send, self.recv = send, recv
        self.me, self.m = lax.axis_index("ctx"), lax.axis_index("mp")
        self.z, self.y = lax.div(self.me, ny), lax.rem(self.me, ny)
        self.slots, self.started = 0, []

    def y_of(self, k):
        return lax.rem(self.y + k + self.ny, self.ny)

    def z_of(self, k):
        return lax.rem(self.z + k + self.nz, self.nz)

    def m_of(self, k):
        return lax.rem(self.m + k, self.n_mp)

    def at_y(self, k):
        return (self.z * self.ny + self.y_of(k), self.m)

    def at_z(self, k):
        return (self.z_of(k) * self.ny + self.y, self.m)

    def at_m(self, k):
        return (self.me, self.m_of(k))

    def at_ctx(self, k):
        return (lax.rem(self.me + k + self.n_ctx, self.n_ctx), self.m)

    def greet(self):
        barrier = pltpu.get_barrier_semaphore()
        peers = [self.at_y(k) for k in range(1, self.ny)]
        peers += [self.at_z(k) for k in range(1, self.nz)]
        peers += [self.at_m(k) for k in range(1, self.n_mp)]
        peers += [self.at_ctx(1), self.at_ctx(-1)]
        for peer in peers:
            pl.semaphore_signal(barrier, inc=1, device_id=peer, device_id_type=MESH)
        return lambda: pl.semaphore_wait(barrier, len(peers))

    def take(self, count):
        first = self.slots
        self.slots += count
        return first

    def copy(self, src, dst, slot, peer):
        return pltpu.make_async_remote_copy(
            src_ref=src,
            dst_ref=dst,
            send_sem=self.send.at[slot],
            recv_sem=self.recv.at[slot],
            device_id=peer,
            device_id_type=MESH,
        )

    def go(self, src, dst, peer):
        made = self.copy(src, dst, self.take(1), peer)
        made.start()
        self.started.append(made)
        return made

    def finish(self):
        for made in self.started:
            made.wait_send()


def arrived(copies):
    for made in copies:
        made.wait_recv()


def ring_start(net, size, place, peer, part):
    if size != 8:
        return [net.go(part(place(0), 2), part(place(0), 2), peer(k)) for k in range(1, size)]
    return [net.go(part(place(0), 2), part(place(0), 2), peer(k)) for k in (2, -2, 1, -1)]


def ring_relay(net, size, place, peer, part, first):
    if size != 8:
        arrived(first)
        return []
    arrived(first[:2])
    made = [
        net.go(part(place(-2), 0), part(place(-2), 0), peer(2)),
        net.go(part(place(2), 1), part(place(2), 1), peer(-2)),
        net.go(part(place(-2), 2), part(place(-2), 2), peer(1)),
        net.go(part(place(2), 2), part(place(2), 2), peer(-1)),
    ]
    return made


def hop_start(net, size, place, peer, part):
    ks = (1, -1) if size == 8 else range(1, size)
    return [net.go(part(place(0), 2), part(place(0), 2), peer(k)) for k in ks]


def hop_next(net, size, place, peer, part, first):
    arrived(first)
    if size != 8:
        return []
    return [net.go(part(place(-k), 2), part(place(-k), 2), peer(k)) for k in (1, -1)]


def hop_last(net, size, place, peer, part, first):
    arrived(first)
    if size != 8:
        return []
    return [
        net.go(part(place(-2), 0), part(place(-2), 0), peer(2)),
        net.go(part(place(2), 1), part(place(2), 1), peer(-2)),
        net.go(part(place(-2), 2), part(place(-2), 2), peer(1)),
        net.go(part(place(2), 2), part(place(2), 2), peer(-1)),
    ]


def cut(ref, size, axis, lanes):
    def part(origin, which):
        span = pl.ds(0, size) if which == 2 else pl.ds(which * (size // 2), size // 2)
        if axis == "z":
            return ref.at[origin, span, :, lanes]
        return ref.at[span, origin, :, lanes]

    return part


def mega_kernel(nz, ny, n_ctx, n_mp, names, *refs):
    r = dict(zip(names, refs))
    net = Net(nz, ny, n_ctx, n_mp, r["send"], r["recv"])
    z, y, m = net.z, net.y, net.m
    seq_ref, alog_ref, skip_ref = r["seq"], r["alog"], r["skip"]
    tokens, width = seq_ref.shape
    tics, groups = tokens // CHUNKS, width // LANES
    half_width = width // 2
    row = chunk_row()
    g_ref, gg_ref, x_ref = r["g"], r["gg"], r["x"]
    wo_ref, do_ref = r["w_all"], r["d_all"]
    net.greet()()

    w_cut = 2 * LANES
    w_lo, w_hi = pl.ds(0, w_cut), pl.ds(w_cut, PROJ - w_cut)
    d_lo, d_hi = pl.ds(0, half_width), pl.ds(half_width, half_width)

    def first_leg(src, ref, lo, hi):
        a = [net.go(src.at[:, lo], ref.at[z, y, :, lo], net.at_y(k)) for k in range(1, ny)]
        b = [net.go(src.at[:, hi], ref.at[z, y, :, hi], net.at_z(k)) for k in range(1, nz)]
        return a, b

    def legs(ref, lo, hi):
        return (
            (nz, net.z_of, net.at_z, cut(ref, ny, "z", lo)),
            (ny, net.y_of, net.at_y, cut(ref, nz, "y", hi)),
        )

    w_za, w_yb = legs(wo_ref, w_lo, w_hi)
    d_za, d_yb = legs(do_ref, d_lo, d_hi)
    w_a, w_b = first_leg(r["w"], wo_ref, w_lo, w_hi)
    halo = net.go(seq_ref.at[pl.ds(tokens - 16, 16)], r["halo"], net.at_ctx(1))
    d_a, d_b = first_leg(r["d"], do_ref, d_lo, d_hi)
    perm = permutation(tokens)
    signed = (perm * -r["flag"][...].astype(F32)).astype(BF16)
    perm = perm.astype(BF16)
    x_ref[...] = dot(perm, seq_ref[...])
    g_ref[...] = dot(perm, r["gate"][...])
    gg_ref[...] = dot(signed, r["up"][...])
    wo_ref[z, y] = r["w"][...]
    do_ref[z, y] = r["d"][...]
    arrived(w_a)
    w_a = ring_start(net, *w_za)
    arrived(w_b)
    w_b = ring_start(net, *w_yb)
    arrived(d_a)
    d_a = hop_start(net, *d_za)
    arrived(d_b)
    d_b = hop_start(net, *d_yb)
    halo.wait_recv()
    first_block = net.me == 0
    act_ref, pre_ref, actb_ref = r["act"], r["pre"], r["actb"]

    def conv(g, carry):
        at = lanes_of(g)
        x = stacked(x_ref[:, at])
        edge = jnp.where(first_block, 0.0, r["halo"][:, at].astype(F32))
        padded = with_earlier(x, edge, CONV - 1)
        taps = r["cw"][:, at]
        pre = r["cb"][:, at][None] + taps[0:1][None] * padded[: x.shape[0]]
        for k in range(1, CONV):
            pre = pre + taps[k : k + 1][None] * padded[k : k + x.shape[0]]
        pre = flat(pre)
        act = (pre * sigmoid(pre)).astype(BF16)
        pre_ref[:, at] = pre
        actb_ref[:, at] = act
        act_ref[:, at] = act.astype(F32)
        return carry

    def gates(g, carry):
        at = lanes_of(g)
        gate = g_ref[:, at]
        out = gg_ref[:, at]
        s = sigmoid(gate)
        g_ref[:, at] = out * (gate * s)
        gg_ref[:, at] = out * (s * (1.0 + gate * (1.0 - s)))
        return carry

    lax.fori_loop(0, groups, conv, 0)
    lax.fori_loop(0, groups, gates, 0)
    w_a2 = ring_relay(net, *w_za, w_a)
    w_b2 = ring_relay(net, *w_yb, w_b)
    d_a = hop_next(net, *d_za, d_a)
    d_b = hop_next(net, *d_yb, d_b)
    if nz == 8:
        arrived(w_a[2:])
    if ny == 8:
        arrived(w_b[2:])
    arrived(w_a2 + w_b2)

    sum_shape = (n_mp, tokens // n_mp, PROJ)
    w_full = wo_ref[...].reshape(width, PROJ)
    r["p1"][...] = dot(actb_ref[...], w_full).astype(BF16).reshape(sum_shape)

    def sum_start(p_ref, r_ref):
        return [net.go(p_ref.at[net.m_of(k)], r_ref.at[k], net.at_m(k)) for k in range(1, n_mp)]

    def sum_turn(first, p_ref, r_ref, acc_ref, o_ref):
        total = p_ref[m].astype(F32)
        for k in range(1, n_mp):
            first[k - 1].wait_recv()
            total = total + r_ref[k].astype(F32)
        acc_ref[...] = total.astype(BF16)
        o_ref[m] = acc_ref[...]
        return [net.go(acc_ref, o_ref.at[m], net.at_m(k)) for k in range(1, n_mp)]

    s1 = sum_start(r["p1"], r["q1"])
    d_a = hop_last(net, *d_za, d_a)
    d_b = hop_last(net, *d_yb, d_b)
    s2 = sum_turn(s1, r["p1"], r["q1"], r["acc1"], r["proj"])
    arrived(d_a + d_b)

    def lay_out(i, carry):
        rows = do_ref.shape[2] * ny
        block = do_ref[i].astype(F32).reshape(rows, width)
        r["dt"][pl.ds(pl.multiple_of(i * rows, rows), rows)] = block.astype(BF16)
        return carry

    lax.fori_loop(0, nz, lay_out, 0)
    dt_ref = r["dt"]
    arrived(s2)

    proj = r["proj"][...].reshape(tokens, PROJ)
    low = proj[:, :RANK]
    cols = proj[:, RANK:].astype(F32)
    step_ref, sig_ref = r["step"], r["sig"]
    step_ref[...] = dot(low, dt_ref[...])
    b_ref, c_ref = r["b"], r["c"]

    def spread(first, out_ref):
        for n in range(STATE):
            col = cols[:, first + n : first + n + 1]
            out_ref[:, n] = stacked(jnp.broadcast_to(col, (tokens, LANES)))

    spread(0, b_ref)
    spread(STATE, c_ref)
    rx_ref, row_ref, rz_ref, back_ref, edge_ref = r["rx"], r["rowt"], r["rz"], r["backt"], r["edges"]
    decay_ref = r["decay"]
    pe_ref, pq_ref, pack_ref, ends_ref = r["pe"], r["pq"], r["pack"], r["ends"]
    wide = (STATE, CHUNKS, LANES)
    base1 = net.take(ny)

    def pack_copy(k):
        peer = (z * ny + lax.rem(y + k, ny), m)
        return net.copy(pack_ref.at[lax.rem(y + k, ny)], rx_ref.at[y], base1 + k, peer)

    def here_of(t):
        return pl.ds(pl.multiple_of(t * CHUNKS, CHUNKS), CHUNKS)

    run_ref, total_ref, wl_ref, wr_ref = r["run"], r["total"], r["wl"], r["wr"]

    def others(total):
        left, right = total, total
        shift = 1
        while shift < CHUNKS:
            left = left + jnp.where(row >= shift, pltpu.roll(left, shift, 1), 0.0)
            right = right + jnp.where(
                row < CHUNKS - shift, pltpu.roll(right, CHUNKS - shift, 1), 0.0
            )
            shift *= 2
        before = jnp.where(row >= 1, pltpu.roll(left, 1, 1), 0.0)
        after = jnp.where(row < CHUNKS - 1, pltpu.roll(right, CHUNKS - 1, 1), 0.0)
        return before, after

    def settle(g, carry):
        at = lanes_of(g)
        a2 = jnp.broadcast_to((-LOG2E * jnp.exp(alog_ref[:, at]))[:, None, :], wide)
        earlier, later = others(total_ref[:, at][None])
        wl_ref[:, :, at] = jnp.exp2(a2 * earlier)
        wr_ref[:, :, at] = jnp.exp2(a2 * later)
        state, adjoint, left = pe_ref[:, :, at], pq_ref[:, :, at], run_ref[:, :, at]
        right = left
        shift = 1
        while shift < CHUNKS:
            in_left = row >= shift
            in_right = row < CHUNKS - shift
            state = state + left * jnp.where(in_left, pltpu.roll(state, shift, 1), 0.0)
            left = left * jnp.where(in_left, pltpu.roll(left, shift, 1), 1.0)
            adjoint = adjoint + right * jnp.where(
                in_right, pltpu.roll(adjoint, CHUNKS - shift, 1), 0.0
            )
            right = right * jnp.where(in_right, pltpu.roll(right, CHUNKS - shift, 1), 1.0)
            shift *= 2
        pe_ref[:, :, at] = jnp.where(row >= 1, pltpu.roll(state, 1, 1), 0.0)
        pq_ref[:, :, at] = jnp.where(row < CHUNKS - 1, pltpu.roll(adjoint, CHUNKS - 1, 1), 0.0)
        return carry

    def local(i, carry):
        k = lax.rem(i + 1, ny)
        g = lax.rem(y + k, ny)
        at = lanes_of(g)
        pre = step_ref[:, at] + r["dbias"][:, at]
        step_ref[:, at] = jnp.maximum(pre, 0.0) + jnp.log1p(jnp.exp(-jnp.abs(pre)))
        sig_ref[:, at] = pre
        a2 = jnp.broadcast_to((-LOG2E * jnp.exp(alog_ref[:, at]))[:, None, :], wide)

        def ahead(t, carry):
            state, adjoint, run, total = carry
            here = here_of(t)
            step = step_ref[here, at]
            flow = step * act_ref[here, at]
            decay = jnp.exp2(step[None] * a2)
            decay_ref[g, t] = decay
            run = run * decay
            state = decay * state + b_ref[t] * flow[None]
            adjoint = adjoint + run * (c_ref[t] * g_ref[here, at][None])
            return state, adjoint, run, total + step

        zero = jnp.zeros(wide, F32)
        state, adjoint, left, total = lax.fori_loop(
            0,
            tics,
            ahead,
            (zero, zero, jnp.ones(wide, F32), jnp.zeros((CHUNKS, LANES), F32)),
            unroll=UNROLL_L,
        )
        pe_ref[:, :, at] = state
        pq_ref[:, :, at] = adjoint
        run_ref[:, :, at] = left
        total_ref[:, at] = total
        earlier, later = others(total[None])
        ends_ref[pl.ds(0, STATE)] = jnp.sum(state * jnp.exp2(a2 * later), axis=1)
        ends_ref[pl.ds(STATE, STATE)] = jnp.sum(adjoint * jnp.exp2(a2 * earlier), axis=1)
        pack_ref[g, pl.ds(0, 2 * STATE)] = ends_ref[...].astype(BF16)
        pack_ref[g, pl.ds(2 * STATE, STATE)] = split_total(jnp.sum(total, axis=0, keepdims=True))

        @pl.when(i < ny - 1)
        def _():
            pack_copy(k).start()

        return carry

    lax.fori_loop(0, groups, local, 0)

    fw_ref, bw_ref = r["fw"], r["bw"]
    rx_ref[y] = pack_ref[y]
    my_a2 = -LOG2E * jnp.exp(alog_ref[:, lanes_of(y)])
    gb_ref, gc_ref = r["gb"], r["gc"]
    r["low_t"][...] = low.astype(F32).T.astype(BF16)

    def slopes(g, carry):
        at = lanes_of(g)
        sig_ref[:, at] = sigmoid(sig_ref[:, at])
        return carry

    lax.fori_loop(0, groups, slopes, 0)
    gb_ref[...] = jnp.zeros(gb_ref.shape, F32)
    gc_ref[...] = jnp.zeros(gc_ref.shape, F32)
    arrived([pack_copy(k) for k in range(1, ny)])

    def total_of(block):
        tail = block[2 * STATE :].astype(F32)
        return tail[0:1] + tail[CHUNKS : CHUNKS + 1]

    zero = jnp.zeros((STATE, LANES), F32)
    totals = [total_of(rx_ref[j]) for j in range(ny)]
    forward, sums = zero, jnp.zeros((1, LANES), F32)
    before, behind = [], [None] * ny
    for j in range(ny):
        fw_ref[j] = forward
        before.append(sums)
        forward = jnp.exp2(my_a2 * totals[j]) * forward + rx_ref[j, pl.ds(0, STATE)].astype(F32)
        sums = sums + totals[j]
    backward, tail_sum = zero, jnp.zeros((1, LANES), F32)
    for j in reversed(range(ny)):
        bw_ref[j] = backward
        behind[j] = tail_sum
        backward = jnp.exp2(my_a2 * totals[j]) * backward + rx_ref[j, pl.ds(STATE, STATE)].astype(F32)
        tail_sum = tail_sum + totals[j]
    row_ref[pl.ds(0, STATE)] = forward.astype(BF16)
    row_ref[pl.ds(STATE, STATE)] = backward.astype(BF16)
    row_ref[pl.ds(2 * STATE, STATE)] = split_total(sums)
    c2 = [net.go(row_ref, rz_ref.at[z], net.at_z(k)) for k in range(1, nz)]
    rz_ref[z] = row_ref[...]
    lax.fori_loop(0, groups, settle, 0)
    arrived(c2)
    head, tail = zero, zero
    for k in range(nz):
        block = rz_ref[k]
        fresh = jnp.exp2(my_a2 * total_of(block)) * head + block[:STATE].astype(F32)
        head = jnp.where(k < z, fresh, head)
    for k in reversed(range(nz)):
        block = rz_ref[k]
        fresh = jnp.exp2(my_a2 * total_of(block)) * tail + block[STATE : 2 * STATE].astype(F32)
        tail = jnp.where(k > z, fresh, tail)
    for j in range(ny):
        into = fw_ref[j] + jnp.exp2(my_a2 * before[j]) * head
        outof = bw_ref[j] + jnp.exp2(my_a2 * behind[j]) * tail
        back_ref[j, pl.ds(0, STATE)] = into.astype(BF16)
        back_ref[j, pl.ds(STATE, STATE)] = outof.astype(BF16)
    base3 = net.take(ny)

    def edge_copy(k):
        peer = (z * ny + lax.rem(y + k, ny), m)
        return net.copy(back_ref.at[lax.rem(y + k, ny)], edge_ref.at[y], base3 + k, peer)

    edge_ref[y] = back_ref[y]
    for k in range(1, ny):
        edge_copy(k).start()

    h_ref, mix_ref, gpre_ref, half_ref = r["h"], r["mix"], r["gpre"], r["half"]
    gas_ref, dw_ref, ra_ref, sg_ref = r["gas"], r["dw"], r["ra"], r["sg"]
    rs_ref, ps_ref = r["rs"], r["ps"]
    flow_ref, slope_ref, low_ref = r["flow"], r["slope"], r["low_sum"]
    low_ref[...] = jnp.zeros(low_ref.shape, F32)
    pairs = groups // 2
    base = net.take(pairs * 16)

    def dw_copy(p, k, along_z):
        if along_z:
            at = lanes_of(2 * p)
            src, peer = dw_ref.at[net.z_of(k), :, :, at], net.at_z(k)
        else:
            at = lanes_of(2 * p + 1)
            src, peer = dw_ref.at[:, net.y_of(k), :, at], net.at_y(k)
        slot = base + p * 16 + k + (0 if along_z else 8)
        return net.copy(src, ra_ref.at[k, :, :, at], slot, peer)

    def main(g):
        at = lanes_of(g)

        @pl.when(g != y)
        def _():
            edge_copy(lax.rem(y - g + ny, ny)).wait_recv()

        a2 = jnp.broadcast_to((-LOG2E * jnp.exp(alog_ref[:, at]))[:, None, :], wide)
        skip = skip_ref[:, at]
        ends = edge_ref[g].astype(F32)
        into = jnp.broadcast_to(ends[:STATE][:, None, :], wide)
        outof = jnp.broadcast_to(ends[STATE:][:, None, :], wide)
        state = pe_ref[:, :, at] + wl_ref[:, :, at] * into
        adjoint = pq_ref[:, :, at] + wr_ref[:, :, at] * outof
        h_ref[0] = state

        def ahead(t, state):
            here = here_of(t)
            step = step_ref[here, at]
            act = act_ref[here, at]
            state = decay_ref[g, t] * state + b_ref[t] * (step * act)[None]
            h_ref[t + 1] = state
            mixed = jnp.sum(c_ref[t] * state, axis=0) + skip * act
            mix_ref[here] = mixed * gg_ref[here, at]
            return state

        lax.fori_loop(0, tics, ahead, state, unroll=UNROLL_F)
        r["mixo"][:, at] = mix_ref[...].astype(BF16)
        none = jnp.zeros((CHUNKS, LANES), F32)
        pre_sum, skip_sum = none, none
        span = STATE // SPLIT
        for part in range(SPLIT):
            of = slice(part * span, part * span + span)
            ns = pl.ds(part * span, span)
            a2_part = a2[of]
            opening, closing = part == 0, part == SPLIT - 1

            def back(i, carry):
                adjoint, rate_sum, pre_sum, skip_sum = carry
                t = tics - 1 - i
                here = here_of(t)
                step = step_ref[here, at]
                act = act_ref[here, at]
                grad = g_ref[here, at]
                lam = c_ref[t, ns] * grad[None] + adjoint
                adjoint = decay_ref[g, t, ns] * lam
                pull = adjoint * h_ref[t, ns]
                gc_ref[t, ns] += h_ref[t + 1, ns] * grad[None]
                gb_ref[t, ns] += lam * (step * act)[None]
                slopes = pull * a2_part
                flow = jnp.sum(lam * b_ref[t, ns], axis=0)
                slope = jnp.sum(slopes, axis=0)
                if not opening:
                    flow = flow + flow_ref[here]
                    slope = slope + slope_ref[here]
                if closing:
                    gas_ref[here, at] = flow * step + skip * grad
                    pre = (flow * act + slope * LN2) * sig_ref[here, at]
                    gpre_ref[here] = pre
                    pre_sum = pre_sum + pre
                    skip_sum = skip_sum + grad * act
                else:
                    flow_ref[here] = flow
                    slope_ref[here] = slope
                return (adjoint, rate_sum + slopes * step[None], pre_sum, skip_sum)

            _, rate_sum, pre_sum, skip_sum = lax.fori_loop(
                0,
                tics,
                back,
                (adjoint[of], jnp.zeros((span, CHUNKS, LANES), F32), pre_sum, skip_sum),
                unroll=UNROLL_B,
            )
            rs_ref[g, ns] = rate_sum
        half_ref[:, at] = gpre_ref[...].astype(BF16)
        ps_ref[g, 0] = pre_sum
        ps_ref[g, 1] = skip_sum

    def gather_sums(g, carry):
        sg_ref[g, pl.ds(0, 1)] = jnp.sum(ps_ref[g, 0], axis=0, keepdims=True)
        sg_ref[g, pl.ds(1, 1)] = jnp.sum(ps_ref[g, 1], axis=0, keepdims=True)
        sg_ref[g, pl.ds(2, CHUNKS - 2)] = jnp.zeros((CHUNKS - 2, LANES), F32)
        sg_ref[g, pl.ds(CHUNKS, STATE)] = LN2 * jnp.sum(rs_ref[g], axis=1)
        return carry

    def main_pair(i, carry):
        turn = lax.rem(i, 2) * (pairs // 2) + lax.div(i, 2)
        p = lax.rem(lax.div(y, 2) + turn, pairs)

        def one(j, carry):
            main(2 * p + lax.rem(y + j, 2))
            return carry

        lax.fori_loop(0, 2, one, 0)
        at = pl.ds(pl.multiple_of(p * 2 * LANES, 2 * LANES), 2 * LANES)
        dw_ref[:, :, :, at] = (
            dot(r["low_t"][...], half_ref[:, at])
            .reshape(dw_ref.shape[:3] + (2 * LANES,))
            .astype(BF16)
        )

        for k in range(1, nz):
            dw_copy(p, k, True).start()
        for k in range(1, ny):
            dw_copy(p, k, False).start()
        low_ref[...] += dot(half_ref[:, at], dt_ref[:, at], ((1,), (1,)))
        return carry

    lax.fori_loop(0, pairs, main_pair, 0)

    pick = jnp.where(
        lax.broadcasted_iota(jnp.int32, (STATE * LANES, STATE), 0) // LANES
        == lax.broadcasted_iota(jnp.int32, (STATE * LANES, STATE), 1),
        1.0,
        0.0,
    ).astype(BF16)

    def folded(ref):
        side = jnp.concatenate([flat(ref[:, n]) for n in range(STATE)], axis=1)
        return dot(side.astype(BF16), pick)

    r["p2"][:, :, pl.ds(0, RANK)] = (
        low_ref[...].astype(BF16).reshape(sum_shape[:2] + (RANK,))
    )
    r["p2"][:, :, pl.ds(RANK, 2 * STATE)] = (
        jnp.concatenate([folded(gb_ref), folded(gc_ref)], axis=1)
        .astype(BF16)
        .reshape(sum_shape[:2] + (2 * STATE,))
    )
    s3 = sum_start(r["p2"], r["q2"])
    lax.fori_loop(0, groups, gather_sums, 0)
    t1 = [net.go(sg_ref.at[net.z_of(k)], r["sr"].at[k], net.at_z(k)) for k in range(1, nz)]
    sa_ref, sb_ref, rra_ref, rrb_ref = r["sa"], r["sb"], r["rra"], r["rrb"]

    def add_a(i, carry):
        for p in range(pairs):
            at, to = pl.ds(2 * p * LANES, LANES), pl.ds(p * LANES, LANES)
            total = dw_ref[z, i, :, at].astype(F32)
            for k in range(1, nz):
                total = total + ra_ref[k, i, :, at].astype(F32)
            sa_ref[i, :, to] = total.astype(BF16)
        return carry

    def add_b(i, carry):
        for p in range(pairs):
            at, to = pl.ds((2 * p + 1) * LANES, LANES), pl.ds(p * LANES, LANES)
            total = dw_ref[i, y, :, at].astype(F32)
            for k in range(1, ny):
                total = total + ra_ref[k, i, :, at].astype(F32)
            sb_ref[i, :, to] = total.astype(BF16)
        return carry

    s4 = sum_turn(s3, r["p2"], r["q2"], r["acc2"], r["gproj"])
    arrived([dw_copy(p, k, True) for p in range(pairs) for k in range(1, nz)])
    lax.fori_loop(0, ny, add_a, 0)
    a2nd = [net.go(sa_ref.at[net.y_of(k)], rra_ref.at[k], net.at_y(k)) for k in range(1, ny)]
    arrived([dw_copy(p, k, False) for p in range(pairs) for k in range(1, ny)])
    lax.fori_loop(0, nz, add_b, 0)
    b2nd = [net.go(sb_ref.at[net.z_of(k)], rrb_ref.at[k], net.at_z(k)) for k in range(1, nz)]
    arrived(t1)
    total = sg_ref[z]
    for k in range(1, nz):
        total = total + r["sr"][k]
    r["ss"][...] = total
    t2 = [net.go(r["ss"], r["srr"].at[k], net.at_y(k)) for k in range(1, ny)]
    arrived(s4)

    out_ref, head_ref, cg_ref = r["grad"], r["head"], r["cg"]
    out_ref[...] = dot(r["gproj"][...].reshape(tokens, PROJ), wo_ref[...].reshape(width, PROJ), ((1,), (1,)))

    rows_ref = r["rows"]
    rows_ref[...] = jnp.zeros(rows_ref.shape, F32)

    def close(g, carry):
        at = lanes_of(g)
        pre = pre_ref[:, at]
        s = sigmoid(pre)
        grad = (gas_ref[:, at] + out_ref[:, at]) * (s * (1.0 + pre * (1.0 - s)))
        out_ref[:, at] = grad
        grad = stacked(grad)
        edge = jnp.where(first_block, 0.0, r["halo"][:, at].astype(F32))
        x = stacked(x_ref[:, at])
        padded = with_earlier(x, edge, CONV - 1)
        for k in range(CONV):
            part = jnp.sum(grad * padded[k : k + x.shape[0]], axis=0)
            rows_ref[pl.ds(k, 1)] = jnp.sum(part, axis=0, keepdims=True)
        rows_ref[pl.ds(CONV, 1)] = jnp.sum(jnp.sum(grad, axis=0), axis=0, keepdims=True)
        cg_ref[g] = rows_ref[...].astype(BF16)
        head_ref[:, at] = jnp.zeros((CHUNKS, LANES), F32)
        for k in range(CONV - 1):
            head_ref[pl.ds(k, 1), at] = grad[k, 0:1]
        return carry

    lax.fori_loop(0, groups, close, 0)
    later = net.go(head_ref, r["later"], net.at_ctx(-1))
    u1 = [net.go(cg_ref.at[net.z_of(k)], r["cr"].at[k], net.at_z(k)) for k in range(1, nz)]
    arrived(a2nd)
    total = sa_ref[y].astype(F32)
    for k in range(1, ny):
        total = total + rra_ref[k].astype(F32)
    for p in range(pairs):
        r["dwo"][:, pl.ds(2 * p * LANES, LANES)] = total[:, p * LANES : (p + 1) * LANES]
    arrived(b2nd)
    total = sb_ref[z].astype(F32)
    for k in range(1, nz):
        total = total + rrb_ref[k].astype(F32)
    for p in range(pairs):
        r["dwo"][:, pl.ds((2 * p + 1) * LANES, LANES)] = total[:, p * LANES : (p + 1) * LANES]
    arrived(t2)
    total = r["ss"][...]
    for k in range(1, ny):
        total = total + r["srr"][k]
    r["smallo"][pl.ds(CHUNKS, 24)] = total
    arrived(u1)
    total = cg_ref[z].astype(F32)
    for k in range(1, nz):
        total = total + r["cr"][k].astype(F32)
    r["cs"][...] = total.astype(BF16)
    u2 = [net.go(r["cs"], r["crr"].at[k], net.at_y(k)) for k in range(1, ny)]
    later.wait_recv()
    last_block = net.me == n_ctx - 1

    def conv_back(g, carry):
        at = lanes_of(g)
        grad = stacked(out_ref[:, at])
        edge = jnp.where(last_block, 0.0, r["later"][:, at])
        rest = pltpu.roll(grad[: CONV - 1], CHUNKS - 1, 1)
        rest = jnp.where(row == CHUNKS - 1, edge[: CONV - 1][:, None, :], rest)
        padded = jnp.concatenate([grad, rest], axis=0)
        taps = r["cw"][:, at]
        total = taps[CONV - 1 :][None] * grad
        for k in range(CONV - 1):
            off = CONV - 1 - k
            total = total + taps[k : k + 1][None] * padded[off : off + grad.shape[0]]
        r["seqo"][:, at] = flat(total).astype(BF16)
        return carry

    lax.fori_loop(0, groups, conv_back, 0)
    for k in range(1, ny):
        pack_copy(k).wait_send()
        edge_copy(k).wait_send()
    for p in range(pairs):
        for k in range(1, nz):
            dw_copy(p, k, True).wait_send()
        for k in range(1, ny):
            dw_copy(p, k, False).wait_send()
    arrived(u2)
    total = r["cs"][...].astype(F32)
    for k in range(1, ny):
        total = total + r["crr"][k].astype(F32)
    r["smallo"][pl.ds(0, CHUNKS)] = total
    net.finish()


def end_kernel(
    ny,
    seq_ref,
    mix_ref,
    dwo_ref,
    small_ref,
    out_ref,
    gate_ref,
    dw_ref,
    w_ref,
    b_ref,
    t_ref,
    a_ref,
    s_ref,
):
    tokens, width = seq_ref.shape
    me = lax.axis_index("ctx")
    unperm = permutation(tokens, True).astype(BF16)
    out_ref[...] = dot(unperm, seq_ref[...]).astype(BF16)
    gate_ref[...] = dot(unperm, mix_ref[...]).astype(BF16)
    dw_ref[...] = dwo_ref[...]
    share = LANES // ny
    shift = lax.rem(LANES - lax.rem(me, ny) * share, LANES)
    mine = pltpu.roll(small_ref[...], shift, 1)[:, :share]
    w_ref[...] = mine[:CONV]
    b_ref[...] = mine[CONV : CONV + 1]
    t_ref[...] = mine[CHUNKS : CHUNKS + 1]
    s_ref[...] = mine[CHUNKS + 1 : CHUNKS + 2]
    a_ref[...] = mine[2 * CHUNKS :]


def body(
    ny,
    seq_in,
    gate_in,
    upstream,
    forget_flags,
    conv_weight,
    conv_bias,
    proj_weight,
    dt_weight,
    dt_bias,
    a_log,
    skip_gain,
):
    n_ctx, n_mp = lax.axis_size("ctx"), lax.axis_size("mp")
    nz = n_ctx // ny
    tokens, width = seq_in.shape
    tics, groups = tokens // CHUNKS, width // LANES
    rows, half, most = dt_weight.shape[0], width // 2, max(nz, ny)
    full, wide = (tokens, width), (tics, STATE, CHUNKS, LANES)
    line = (1, width)
    inputs = dict(
        seq=seq_in,
        gate=gate_in,
        up=upstream,
        flag=forget_flags.reshape(1, tokens),
        cw=conv_weight,
        cb=conv_bias.reshape(line),
        w=proj_weight,
        d=dt_weight,
        dbias=dt_bias.reshape(line),
        alog=a_log,
        skip=skip_gain.reshape(line),
    )
    outs = dict(
        seqo=(full, BF16),
        mixo=(full, BF16),
        dwo=((rows, width), F32),
        smallo=((24 + CHUNKS, LANES), F32),
    )
    part = (n_mp, tokens // n_mp, PROJ)
    scratch = dict(
        x=(full, F32),
        g=(full, F32),
        gg=(full, F32),
        act=(full, F32),
        pre=(full, F32),
        step=(full, F32),
        sig=(full, F32),
        gas=(full, F32),
        actb=(full, BF16),
        half=(full, BF16),
        halo=((16, width), BF16),
        w_all=((nz, ny) + proj_weight.shape, BF16),
        d_all=((nz, ny) + dt_weight.shape, BF16),
        dt=((RANK, width), BF16),
        low_t=((RANK, tokens), BF16),
        p1=(part, BF16),
        q1=(part, BF16),
        acc1=(part[1:], BF16),
        proj=(part, BF16),
        p2=(part, BF16),
        q2=(part, BF16),
        acc2=(part[1:], BF16),
        gproj=(part, BF16),
        b=(wide, F32),
        c=(wide, F32),
        gb=(wide, F32),
        gc=(wide, F32),
        h=((tics + 1,) + wide[1:], F32),
        pe=((STATE, CHUNKS, width), F32),
        pq=((STATE, CHUNKS, width), F32),
        pack=((groups, 3 * STATE, LANES), BF16),
        ends=((2 * STATE, LANES), F32),
        rx=((ny, 3 * STATE, LANES), BF16),
        rowt=((3 * STATE, LANES), BF16),
        rz=((nz, 3 * STATE, LANES), BF16),
        backt=((ny, 2 * STATE, LANES), BF16),
        edges=((groups, 2 * STATE, LANES), BF16),
        fw=((ny, STATE, LANES), F32),
        bw=((ny, STATE, LANES), F32),
        mix=((tokens, LANES), F32),
        gpre=((tokens, LANES), F32),
        dw=((nz, ny, rows, width), BF16),
        ra=((most, most, rows, width), BF16),
        sa=((ny, rows, half), BF16),
        sb=((nz, rows, half), BF16),
        rra=((ny, rows, half), BF16),
        rrb=((nz, rows, half), BF16),
        sg=((groups, 24, LANES), F32),
        sr=((nz, 24, LANES), F32),
        ss=((24, LANES), F32),
        srr=((ny, 24, LANES), F32),
        head=((CHUNKS, width), F32),
        later=((CHUNKS, width), F32),
        grad=(full, F32),
        flow=((tokens, LANES), F32),
        low_sum=((tokens, RANK), F32),
        run=((STATE, CHUNKS, width), F32),
        wl=((STATE, CHUNKS, width), F32),
        wr=((STATE, CHUNKS, width), F32),
        total=((CHUNKS, width), F32),
        rs=((groups, STATE, CHUNKS, LANES), F32),
        ps=((groups, 2, CHUNKS, LANES), F32),
        decay=((groups,) + wide, F32),
        slope=((tokens, LANES), F32),
        rows=((CHUNKS, LANES), F32),
        cg=((groups, CHUNKS, LANES), BF16),
        cr=((nz, CHUNKS, LANES), BF16),
        cs=((CHUNKS, LANES), BF16),
        crr=((ny, CHUNKS, LANES), BF16),
    )
    names = list(inputs) + list(outs) + list(scratch) + ["send", "recv"]
    slots = 256
    seq, mix, dwo, small = call(
        functools.partial(mega_kernel, nz, ny, n_ctx, n_mp, names),
        list(outs.values()),
        list(inputs.values()),
        [pltpu.VMEM(s, d) for s, d in scratch.values()]
        + [pltpu.SemaphoreType.DMA((slots,)), pltpu.SemaphoreType.DMA((slots,))],
        1,
    )
    share = LANES // ny
    grad_seq, grad_gate, grad_dtw, g_w, g_b, g_t, g_a, g_s = call(
        functools.partial(end_kernel, ny),
        [
            (full, BF16),
            (full, BF16),
            ((rows, width), F32),
            ((CONV, share), F32),
            ((1, share), F32),
            ((1, share), F32),
            ((STATE, share), F32),
            ((1, share), F32),
        ],
        [seq, mix, dwo, small],
    )
    return (
        grad_seq,
        grad_gate,
        grad_dtw,
        g_w,
        g_b.reshape(share),
        g_t.reshape(share),
        g_a,
        g_s.reshape(share),
    )


def build(mesh, ny):
    return jax.shard_map(
        functools.partial(body, ny),
        mesh=mesh,
        in_specs=(
            P("ctx", "mp"),
            P("ctx", "mp"),
            P("ctx", "mp"),
            P("ctx"),
            P(None, "mp"),
            P("mp"),
            P(("mp", "ctx"), None),
            P("ctx", "mp"),
            P("mp"),
            P(None, "mp"),
            P("mp"),
        ),
        out_specs=(
            P("ctx", "mp"),
            P("ctx", "mp"),
            P("ctx", "mp"),
            P(None, ("mp", "ctx")),
            P(("mp", "ctx")),
            P(("mp", "ctx")),
            P(None, ("mp", "ctx")),
            P(("mp", "ctx")),
        ),
        check_vma=False,
    )


def solution(mesh):
    return build(mesh, NY)
```
